256 devices in a mesh: seq: 32 (over x, y, core), head: 8 (over z).
Axes of the slice: x: 4, y: 4, z: 8, core: 2. Of those that a mesh axis runs over, the one named last changes fastest.
Arguments:
- projected: bfloat16 [49152, 6912], P(('seq', 'head')), may hold values from -10 to 10
- segment_ids: int32 [49152], replicated, may hold values from 0 to 63, never falling along the last dimension, each value on 1 to 1536 neighbouring positions
- widths: int32 [64], replicated, may hold values from 16 to 64
Outputs:
- attended: bfloat16 [49152, 2304], P(('seq', 'head'))
The draws below stay inside these ranges and needn't reach their ends.
Inputs may be any that keep to these rules, and one draw needn't show every extreme that they name: `segment_ids`: ids never fall along the sequence; each of the 64 samples covers 1 to 1536 consecutive positions and some sample covers exactly 1536.
All inputs are finite; a program needn't handle non-finite values.
Results may differ from the reference program's by a relative error of at most 0.0088.
Values may be sent and summed in bfloat16 or wider, within the bound.
No kernel may reach another device: no remote copies, remote signals or barrier semaphores. Data moves between devices by JAX's collectives and lax.ppermute only.
A program may use at most 128 MiB of HBM per device.

```python
import math
import jax
import jax.numpy as jnp
import numpy as np
from jax import lax

D = 2304
HEADS = 24
MAXLEN = 1536
TOKENS = 49152
SAMPLES = 64


def draw_projected(key, part):
    head_size = D // HEADS
    base_key = jax.random.fold_in(key, 11)
    shape = (TOKENS, 3, HEADS, head_size)
    stacked = jnp.clip(jax.random.normal(base_key, shape, jnp.float32), -5.0, 5.0)
    return stacked.reshape(TOKENS, 3 * D).astype(jnp.bfloat16)


def with_ends(result, stream_key, smallest, largest):
    shape = result.shape
    spot = [jax.random.randint(jax.random.fold_in(stream_key, axis), (), 0, shape[axis]) for axis in range(len(shape))]
    result = result.at[tuple(spot)].set(smallest)
    longest = shape.index(max(shape))
    spot[longest] = (spot[longest] + 1) % shape[longest]
    return result.at[tuple(spot)].set(largest)


def split_up(count, total, reach, skew):
    portions = [(1 << 20) // math.isqrt(standing ** skew) + 1 for standing in range(2, count + 1)]
    spare, counts = total - reach - (count - 1), [1] * (count - 1)
    while spare > 0:
        movable = [i for i in range(count - 1) if counts[i] < reach]
        pool, budget = sum([portions[i] for i in movable]), spare
        for i in movable:
            addition = min(reach - counts[i], max(1, budget * portions[i] // pool), spare)
            counts[i] = counts[i] + addition
            spare = spare - addition
    return np.array([reach] + counts)


def ragged(key, number_of, total, limit, skew):
    if number_of == 2:
        one = jax.random.randint(key, (), max(1, total - limit), min(limit, total - 1) + 1)
        return jnp.stack([one, total - one])
    sizes = jnp.asarray(split_up(number_of, total, limit, skew), jnp.int32)
    pairs = (number_of - 1) // 2
    giver, receiver = sizes[1:1 + 2 * pairs:2], sizes[2:2 + 2 * pairs:2]
    slack = jnp.minimum(giver - 1, limit - receiver)
    shifted = jax.random.randint(jax.random.fold_in(key, 1), (pairs,), 0, 1 << 20) % (slack + 1)
    sizes = sizes.at[1:1 + 2 * pairs:2].set(giver - shifted).at[2:2 + 2 * pairs:2].set(receiver + shifted)
    return sizes[jax.random.permutation(jax.random.fold_in(key, 2), number_of)]


def setup_inputs(seed: int = 0) -> dict:
    key_list = jax.random.split(jax.random.key(seed), 4)
    projected = draw_projected(jax.random.fold_in(key_list[3], 71), 0)
    segment_ids = jnp.searchsorted(jnp.cumsum(ragged(key_list[1], SAMPLES, TOKENS, MAXLEN, 2)), jnp.arange(TOKENS), side="right").astype(jnp.int32)
    widths = with_ends(jax.random.randint(key_list[2], (SAMPLES,), 16, 65), jax.random.fold_in(key_list[2], 1), 16, 64).astype(jnp.int32)
    return dict(projected=projected, segment_ids=segment_ids, widths=widths)


masked_score = -1e+30

def rotate(head_vals, row_pos, col_pos):
    quarter = head_vals.shape[-1] // 4
    frequency = 10000.0 ** (-jnp.arange(quarter, dtype=jnp.float32) / quarter)

    def turn(half_vals, place):
        angles = place.astype(jnp.float32)[:, None] * frequency[None, :]
        cosine = jnp.cos(angles)[:, None, :]
        sine_part = jnp.sin(angles)[:, None, :]
        first_half = half_vals[..., :quarter]
        second = half_vals[..., quarter:]
        return jnp.concatenate([first_half * cosine - second * sine_part, first_half * sine_part + second * cosine], axis=-1)
    middle = 2 * quarter
    return jnp.concatenate([turn(head_vals[..., :middle], row_pos), turn(head_vals[..., middle:], col_pos)], axis=-1)

def starts_of(segment_ids):
    length = segment_ids.shape[0]
    indices = jnp.arange(length, dtype=jnp.int32)
    before = jnp.concatenate([jnp.full((1,), -1, jnp.int32), segment_ids[:-1]])
    return lax.cummax(jnp.where(segment_ids != before, indices, 0), axis=0)

def reference(projected, segment_ids, widths):
    tokens = projected.shape[0]
    head_size = D // HEADS
    indices = jnp.arange(tokens, dtype=jnp.int32)
    offset = indices - starts_of(segment_ids)
    width_tok = widths[segment_ids]
    row_pos = offset // width_tok
    col_pos = offset % width_tok
    qkv_parts = projected.reshape(tokens, 3, HEADS, head_size)
    queries = rotate(qkv_parts[:, 0].astype(jnp.float32), row_pos, col_pos).astype(jnp.bfloat16)
    key_rows = rotate(qkv_parts[:, 1].astype(jnp.float32), row_pos, col_pos).astype(jnp.bfloat16)
    values = qkv_parts[:, 2]
    reach_rows = MAXLEN
    zero_rows = jnp.zeros((reach_rows, HEADS, head_size), jnp.bfloat16)
    key_pad = jnp.concatenate([zero_rows, key_rows, zero_rows], axis=0)
    value_pad = jnp.concatenate([zero_rows, values, zero_rows], axis=0)
    no_sample = jnp.full((reach_rows,), -1, jnp.int32)
    seg_pad = jnp.concatenate([no_sample, segment_ids, no_sample], axis=0)
    block_rows = min(512, tokens)
    scaling = 1.0 / math.sqrt(head_size)

    def one_block(number):
        start_row = number * block_rows
        q_blk = lax.dynamic_slice_in_dim(queries, start_row, block_rows, 0).astype(jnp.float32)
        k_blk = lax.dynamic_slice_in_dim(key_pad, start_row, block_rows + 2 * reach_rows, 0).astype(jnp.float32)
        v_blk = lax.dynamic_slice_in_dim(value_pad, start_row, block_rows + 2 * reach_rows, 0).astype(jnp.float32)
        q_ids = lax.dynamic_slice_in_dim(segment_ids, start_row, block_rows, 0)
        k_ids = lax.dynamic_slice_in_dim(seg_pad, start_row, block_rows + 2 * reach_rows, 0)
        scores = jnp.einsum('qhe,khe->hqk', q_blk, k_blk) * scaling
        same_seg = (q_ids[:, None] == k_ids[None, :])[None]
        scores = jnp.where(same_seg, scores, masked_score)
        row_max = lax.optimization_barrier(jnp.max(scores, axis=2, keepdims=True))
        weights = jnp.where(same_seg, jnp.exp(scores - row_max), 0.0)
        totals = lax.optimization_barrier(jnp.sum(weights, axis=2, keepdims=True))
        blended = jnp.einsum('hqk,khe->hqe', weights.astype(jnp.bfloat16).astype(jnp.float32), v_blk)
        return jnp.transpose(blended / totals, (1, 0, 2)).astype(jnp.bfloat16)
    results = lax.map(one_block, jnp.arange(tokens // block_rows, dtype=jnp.int32))
    return results.reshape(tokens, D)
```

```python
import math

import jax
import jax.numpy as jnp
import numpy as np
from jax import lax
from jax.experimental import pallas as pl
from jax.experimental.pallas import tpu as pltpu
from jax.sharding import PartitionSpec as P

D = 2304
HEADS = 24
HD = 96
TOKENS = 49152
SAMPLES = 64
GROUP = 8
SEQ = 32
OWN = 192
SHARD = OWN * GROUP
LANES = 128
SEG_ROWS = TOKENS // LANES
SHARD_ROWS = SHARD // LANES

KV_LANES = 5 * LANES
Q_LANES = 2 * LANES
CODE = 64
BITS = 6
ONE = CODE + 2 * BITS
BIG = float(2**20)
BQ = OWN
BK = 256
MAX_BLOCKS = 14
WINDOW = 3 * SHARD
OUT_ROWS = 2 * OWN + OWN // 4
SCALE = math.log2(math.e) / math.sqrt(HD)


def lane_iota(shape, dtype=jnp.int32):
    return lax.broadcasted_iota(dtype, shape, len(shape) - 1)


def turned(x, amount):
    amount %= LANES
    return x if amount == 0 else pltpu.roll(x, amount, 1)


def pack_kernel(x_ref, seg_ref, widths_ref, freq_ref, kv_ref, q_ref, cos_ref, sin_ref, code_ref):
    device = lax.axis_index("seq") * GROUP + lax.axis_index("head")
    first_tok = device * OWN
    first_row = jnp.maximum(first_tok // LANES - SHARD_ROWS, 0)
    rows = lax.broadcasted_iota(jnp.int32, (OWN, 1), 0)
    lanes = lane_iota((1, LANES))
    window = SHARD_ROWS + 2
    own = jnp.zeros((OWN, LANES), jnp.float32)
    for r in range(window):
        ids = seg_ref[pl.ds(first_row + r, 1), :].astype(jnp.float32)
        place = (first_row + r) * LANES + lanes - first_tok
        own = own + jnp.where(place == rows, ids, 0.0)
    own = jnp.sum(own, axis=1, keepdims=True)
    before = jnp.zeros((OWN, LANES), jnp.float32)
    for r in range(window):
        ids = seg_ref[pl.ds(first_row + r, 1), :].astype(jnp.float32)
        place = (first_row + r) * LANES + lanes - first_tok
        before = before + jnp.where((ids == own) & (place < rows), 1.0, 0.0)
    offset = jnp.sum(before, axis=1, keepdims=True)
    lane_f = lanes.astype(jnp.float32)
    width = jnp.sum(jnp.where(own == lane_f, widths_ref[...].astype(jnp.float32), 0.0), axis=1, keepdims=True)
    row_pos = jnp.floor((offset + 0.5) / width)
    col_pos = offset - row_pos * width
    angle = jnp.where(lanes < HD // 2, row_pos, col_pos) * freq_ref[...]
    first_half = (lanes % (HD // 2)) < HD // 4
    sine = jnp.sin(angle)
    cos_ref[...] = jnp.cos(angle)
    sin_ref[...] = jnp.where(first_half, -sine, sine)
    ids = own.astype(jnp.int32)
    shift = jnp.clip(jnp.where(lanes < CODE + BITS, lanes - CODE, lanes - CODE - BITS), 0, BITS - 1)
    bit = (ids >> shift) & 1
    code = jnp.where(lanes < CODE + BITS, 1 - bit, bit)
    code = jnp.where(lanes == ONE, 1, jnp.where((lanes >= CODE) & (lanes < ONE), code, 0))
    code_ref[...] = code.astype(jnp.float32).astype(jnp.bfloat16)

    step_rows = 32

    def step(i, carry):
        at = pl.ds(pl.multiple_of(i * step_rows, step_rows), step_rows)
        cos = cos_ref[at, :]
        sin = sin_ref[at, :]
        lane = lane_iota((step_rows, LANES))
        first = (lane % (HD // 2)) < HD // 4

        def tile(t):
            return x_ref[at, t * LANES : (t + 1) * LANES]

        def granules(base, count, target):
            t, g = base // LANES, base % LANES
            value = turned(tile(t), target - g)
            if g + 32 * count > LANES:
                cut = target + LANES - g
                value = jnp.where(lane < cut, value, turned(tile(t + 1), target - g))
            return value

        def rope(base):
            x = granules(base, 3, 0).astype(jnp.float32)
            other = jnp.where(first, pltpu.roll(x, LANES - HD // 4, 1), pltpu.roll(x, HD // 4, 1))
            return (x * cos + other * sin).astype(jnp.bfloat16)

        for z in range(GROUP):
            q0 = z * 3 * HD
            k0, v0 = D + q0, 2 * D + q0
            for h in range(3):
                kv_ref[z, at, h * LANES : (h + 1) * LANES] = jnp.where(
                    lane < HD, rope(k0 + h * HD), granules(v0 + 32 * h, 1, HD)
                )
            kv_ref[z, at, 3 * LANES : 4 * LANES] = jnp.where(
                lane < HD, granules(v0 + HD, 3, 0), granules(v0 + 2 * HD, 1, HD)
            )
            q2 = rope(q0 + 2 * HD)
            tail = jnp.where(lane < HD, code_ref[at, :], turned(q2, 32))
            kv_ref[z, at, 4 * LANES : 5 * LANES] = jnp.where(lane < CODE, granules(v0 + 2 * HD + 32, 2, 0), tail)
            q_ref[z, at, :LANES] = jnp.where(lane < HD, rope(q0), turned(q2, HD))
            q_ref[z, at, LANES:] = jnp.where(lane < HD, rope(q0 + HD), turned(q2, 64))
        return carry

    lax.fori_loop(0, OWN // step_rows, step, 0)


def pack(projected, seg_rows, widths_row, freq):
    vmem = pl.BlockSpec(memory_space=pltpu.VMEM)
    return pl.pallas_call(
        pack_kernel,
        out_shape=[
            jax.ShapeDtypeStruct((GROUP, OWN, KV_LANES), jnp.bfloat16),
            jax.ShapeDtypeStruct((GROUP, OWN, Q_LANES), jnp.bfloat16),
        ],
        in_specs=[vmem] * 4,
        out_specs=[vmem] * 2,
        scratch_shapes=[
            pltpu.VMEM((OWN, LANES), jnp.float32),
            pltpu.VMEM((OWN, LANES), jnp.float32),
            pltpu.VMEM((OWN, LANES), jnp.bfloat16),
        ],
        compiler_params=pltpu.CompilerParams(vmem_limit_bytes=40 * 1024 * 1024),
        name="pack",
    )(projected, seg_rows, widths_row, freq)


def attend_kernel(
    prev_ref, own_ref, next_ref, q_ref, seg_ref, out_ref, kv_ref, v0_ref, qa_ref, qc_ref, s_ref, m_ref, o0_ref, o12_ref, lo_ref, hi_ref
):
    shard = lax.axis_index("seq")
    lanes = lane_iota((1, LANES))

    def ids_of(index):
        return seg_ref[pl.ds(pl.multiple_of(index * SHARD_ROWS, 4), SHARD_ROWS), :].astype(jnp.float32)

    own_ids = ids_of(shard)
    prev_ids = jnp.where(shard > 0, ids_of(jnp.maximum(shard - 1, 0)), -1.0)
    next_ids = jnp.where(shard < SEQ - 1, ids_of(jnp.minimum(shard + 1, SEQ - 1)), -1.0)
    place = lax.broadcasted_iota(jnp.int32, (SHARD_ROWS, LANES), 0) * LANES + lane_iota((SHARD_ROWS, LANES))

    def total(x):
        return jnp.sum(jnp.sum(x, axis=0, keepdims=True), axis=1, keepdims=True)

    for b in range(GROUP):
        first = total(jnp.where(place == b * BQ, own_ids, 0.0))
        last = total(jnp.where(place == b * BQ + BQ - 1, own_ids, 0.0))
        low = total(jnp.where(own_ids < first, 1.0, 0.0) - jnp.where(prev_ids == first, 1.0, 0.0))
        high = total(jnp.where(own_ids <= last, 1.0, 0.0) + jnp.where(next_ids == last, 1.0, 0.0))
        lo_ref[b] = low[0, 0].astype(jnp.int32) + SHARD
        hi_ref[b] = high[0, 0].astype(jnp.int32) + SHARD

    chunk = LANES
    first_chunk = lo_ref[0] // chunk
    last_chunk = (hi_ref[GROUP - 1] + BK + chunk - 1) // chunk

    def copy_from(ref, number):
        begin = jnp.clip(first_chunk, number * SHARD_ROWS, (number + 1) * SHARD_ROWS)
        end = jnp.clip(last_chunk, number * SHARD_ROWS, (number + 1) * SHARD_ROWS)

        def move(i, carry):
            src = pl.ds(pl.multiple_of((i - number * SHARD_ROWS) * chunk, chunk), chunk)
            dst = pl.ds(pl.multiple_of(i * chunk, chunk), chunk)
            lane = lane_iota((chunk, LANES))
            parts = []
            for t in range(5):
                value = ref[src, t * LANES : (t + 1) * LANES]
                kv_ref[dst, t * LANES : (t + 1) * LANES] = value
                parts.append(value)
            v0 = jnp.where(lane < 32, turned(parts[0], 32), jnp.where(lane < 64, turned(parts[1], 64), turned(parts[2], 96)))
            v0_ref[dst, :] = jnp.where(lane < HD, v0, jnp.where(lane == HD, 1.0, 0.0).astype(jnp.bfloat16))
            return carry

        lax.fori_loop(begin, end, move, 0)

    copy_from(prev_ref, 0)
    copy_from(own_ref, 1)
    copy_from(next_ref, 2)

    def prepare(b, carry):
        at = pl.ds(pl.multiple_of(b * BQ, BQ), BQ)
        lane = lane_iota((BQ, LANES))
        zero = jnp.zeros((BQ, LANES), jnp.bfloat16)
        t4 = own_ref[at, 4 * LANES :]
        t5 = q_ref[at, :LANES]
        t6 = q_ref[at, LANES:]
        qa_ref[0, at, :] = jnp.where(lane < HD, t5, zero)
        qa_ref[1, at, :] = jnp.where(lane < HD, t6, zero)
        q2 = jnp.where(lane < 32, turned(t5, 32), jnp.where(lane < 64, turned(t6, 64), turned(t4, 96)))
        qa_ref[2, at, :] = jnp.where(lane < HD, q2, zero)
        other = (t4.astype(jnp.float32) - 1.0) * BIG
        qc_ref[at, :] = jnp.where((lane >= CODE) & (lane < ONE), other, 0.0).astype(jnp.bfloat16)
        return carry

    lax.fori_loop(0, GROUP, prepare, 0)

    def block(b, carry):
        lo, hi = lo_ref[b], hi_ref[b]
        start = lo // LANES * LANES
        count = (hi - start + BK - 1) // BK
        start = jnp.minimum(start, WINDOW - count * BK)
        at = pl.ds(pl.multiple_of(b * BQ, BQ), BQ)
        m_ref[...] = jnp.full_like(m_ref, -3.0e38)
        o0_ref[...] = jnp.zeros_like(o0_ref)
        o12_ref[...] = jnp.zeros_like(o12_ref)

        def scores(j, c):
            keys = pl.ds(pl.multiple_of(start + j * BK, LANES), BK)
            t4 = kv_ref[keys, 4 * LANES :]
            for h in range(3):
                k = jnp.concatenate([kv_ref[keys, h * LANES : (h + 1) * LANES], t4], axis=1)
                q = jnp.concatenate([qa_ref[h, at, :], qc_ref[at, :]], axis=1)
                s = lax.dot_general(q, k, (((1,), (1,)), ((), ())), preferred_element_type=jnp.float32)
                s_ref[j, h] = s
                top = s[:, :LANES]
                for t in range(1, BK // LANES):
                    top = jnp.maximum(top, s[:, t * LANES : (t + 1) * LANES])
                m_ref[h] = jnp.maximum(m_ref[h], top)
            return c

        lax.fori_loop(0, count, scores, 0)
        for h in range(3):
            m_ref[h] = jnp.broadcast_to(jnp.max(m_ref[h], axis=1, keepdims=True) * SCALE, (BQ, LANES))

        def blend(j, c):
            keys = pl.ds(pl.multiple_of(start + j * BK, LANES), BK)
            weights = []
            for h in range(3):
                m = jnp.concatenate([m_ref[h]] * (BK // LANES), axis=1)
                weights.append(jnp.exp2(s_ref[j, h] * SCALE - m).astype(jnp.bfloat16))
            o0_ref[...] += jnp.dot(weights[0], v0_ref[keys, :], preferred_element_type=jnp.float32)
            both = jnp.concatenate(weights[1:], axis=0)
            o12_ref[...] += jnp.dot(both, kv_ref[keys, 3 * LANES :], preferred_element_type=jnp.float32)
            return c

        lax.fori_loop(0, count, blend, 0)

        lane = lane_iota((BQ, LANES))
        o0 = o0_ref[...]
        o0 = o0 / o0[:, HD : HD + 1]
        o1 = o12_ref[:BQ, :LANES] / o12_ref[:BQ, LANES:][:, ONE : ONE + 1]
        o2a, o2b = o12_ref[BQ:, :LANES], o12_ref[BQ:, LANES:]
        t2 = o2b[:, ONE : ONE + 1]
        o2a, o2b = o2a / t2, o2b / t2
        out_ref[b, :OWN, :] = jnp.where(lane < HD, o0, o2a).astype(jnp.bfloat16)
        out_ref[b, OWN : 2 * OWN, :] = jnp.where(lane < HD, o1, turned(o2b, 96)).astype(jnp.bfloat16)
        part = OWN // 4
        lane = lane_iota((part, LANES))
        fold = turned(o2b[:part], 96)
        for g in range(1, 4):
            fold = jnp.where(lane < 32 * g, fold, turned(o2b[g * part : (g + 1) * part], 32 * g - 32))
        out_ref[b, 2 * OWN :, :] = fold.astype(jnp.bfloat16)
        return carry

    lax.fori_loop(0, GROUP, block, 0)


def attend(prev, own, following, queries, seg_rows):
    vmem = pl.BlockSpec(memory_space=pltpu.VMEM)
    return pl.pallas_call(
        attend_kernel,
        out_shape=jax.ShapeDtypeStruct((GROUP, OUT_ROWS, LANES), jnp.bfloat16),
        in_specs=[vmem] * 5,
        out_specs=vmem,
        scratch_shapes=[
            pltpu.VMEM((WINDOW, KV_LANES), jnp.bfloat16),
            pltpu.VMEM((WINDOW, LANES), jnp.bfloat16),
            pltpu.VMEM((3, SHARD, LANES), jnp.bfloat16),
            pltpu.VMEM((SHARD, LANES), jnp.bfloat16),
            pltpu.VMEM((MAX_BLOCKS, 3, BQ, BK), jnp.float32),
            pltpu.VMEM((3, BQ, LANES), jnp.float32),
            pltpu.VMEM((BQ, LANES), jnp.float32),
            pltpu.VMEM((2 * BQ, 2 * LANES), jnp.float32),
            pltpu.SMEM((GROUP,), jnp.int32),
            pltpu.SMEM((GROUP,), jnp.int32),
        ],
        compiler_params=pltpu.CompilerParams(vmem_limit_bytes=40 * 1024 * 1024),
        name="attend",
    )(prev, own, following, queries, seg_rows)


def unpack_kernel(in_ref, out_ref):
    lane = lane_iota((OWN, LANES))
    part = OWN // 4

    def source(z, i):
        if i < 3:
            return in_ref[z, :OWN, :], i
        if i < 6:
            return in_ref[z, OWN : 2 * OWN, :], i - 3
        return in_ref[z, (i - 6) * OWN : (i - 5) * OWN, :], 3

    for t in range(D // LANES):
        value = None
        for g in range(4):
            z, i = divmod(4 * t + g, 9)
            if i == 8:
                pieces = [turned(in_ref[z, 2 * OWN :, :], 32 * (g - p)) for p in range(4)]
                moved = jnp.concatenate(pieces, axis=0)
            else:
                tile, at = source(z, i)
                moved = turned(tile, 32 * (g - at))
            value = moved if value is None else jnp.where(lane < 32 * g, value, moved)
        out_ref[:, t * LANES : (t + 1) * LANES] = value


def unpack(returned):
    vmem = pl.BlockSpec(memory_space=pltpu.VMEM)
    return pl.pallas_call(
        unpack_kernel,
        out_shape=jax.ShapeDtypeStruct((OWN, D), jnp.bfloat16),
        in_specs=[vmem],
        out_specs=vmem,
        compiler_params=pltpu.CompilerParams(vmem_limit_bytes=32 * 1024 * 1024),
        name="unpack",
    )(returned)


def frequencies():
    quarter = HD // 4
    lane = np.arange(LANES)
    return (10000.0 ** (-(lane % quarter).astype(np.float64) / quarter)).astype(np.float32)[None, :]


def body(projected, segment_ids, widths):
    seg_rows = segment_ids.reshape(SEG_ROWS, LANES)
    widths_row = jnp.pad(widths, (0, LANES - SAMPLES)).reshape(1, LANES)
    kv, q = pack(projected, seg_rows, widths_row, jnp.asarray(frequencies()))
    kv = lax.all_to_all(kv, "head", 0, 0, tiled=True)
    kv, q = lax.optimization_barrier((kv, q))
    own = kv.reshape(SHARD, KV_LANES)
    up = [(i, (i + 1) % SEQ) for i in range(SEQ)]
    down = [(j, i) for i, j in up]
    prev = lax.ppermute(own, "seq", up)
    following = lax.ppermute(own, "seq", down)
    q = lax.all_to_all(q, "head", 0, 0, tiled=True)
    out = attend(prev, own, following, q.reshape(SHARD, Q_LANES), seg_rows)
    out = lax.all_to_all(out, "head", 0, 0, tiled=True)
    return unpack(out)


def solution(mesh):
    in_specs = (P(("seq", "head"), None), P(), P())
    out_specs = P(("seq", "head"), None)
    return jax.shard_map(body, mesh=mesh, in_specs=in_specs, out_specs=out_specs, check_vma=False)
```

```python
import math

import jax
import jax.numpy as jnp
import numpy as np
from jax import lax
from jax.experimental import pallas as pl
from jax.experimental.pallas import tpu as pltpu
from jax.sharding import PartitionSpec as P

D = 2304
HEADS = 24
HD = 96
TOKENS = 49152
SAMPLES = 64
GROUP = 8
SEQ = 32
OWN = 192
SHARD = OWN * GROUP
LANES = 128
SEG_ROWS = TOKENS // LANES
SHARD_ROWS = SHARD // LANES

KV_LANES = 5 * LANES
Q_LANES = 2 * LANES
CODE = 64
BITS = 6
ONE = CODE + 2 * BITS
BIG = float(2**20)
BQ = 2 * OWN
BLOCKS = SHARD // BQ
BK = 768
MAX_STEPS = 5
CHUNK = 256
PACK_ROWS = 64
SEG_WINDOW = 24
WINDOW = 3 * SHARD
OUT_ROWS = 2 * OWN + OWN // 4
SCALE = math.log2(math.e) / math.sqrt(HD)


def lane_iota(shape, dtype=jnp.int32):
    return lax.broadcasted_iota(dtype, shape, len(shape) - 1)


def turned(x, amount):
    amount %= LANES
    return x if amount == 0 else pltpu.roll(x, amount, 1)


def id_window(seg_ref, ids_ref, sem):
    first_row = jnp.maximum(device_index() * OWN // LANES - SHARD_ROWS, 0)
    base = pl.multiple_of(jnp.minimum(first_row // 8 * 8, SEG_ROWS - SEG_WINDOW), 8)
    return base, pltpu.make_async_copy(seg_ref.at[pl.ds(base, SEG_WINDOW), :], ids_ref, sem)


def device_index():
    return lax.axis_index("seq") * GROUP + lax.axis_index("head")


def row_copies(x_ref, rows_ref, sems):
    count = OWN // PACK_ROWS
    parts = [pl.ds(i * PACK_ROWS, PACK_ROWS) for i in range(count)]
    return [pltpu.make_async_copy(x_ref.at[p, :], rows_ref.at[p, :], sems.at[i]) for i, p in enumerate(parts)]


def swap_matrix():
    source = lax.broadcasted_iota(jnp.int32, (LANES, LANES), 0)
    target = lane_iota((LANES, LANES))
    partner = jnp.where((target % (HD // 2)) < HD // 4, target + HD // 4, target - HD // 4)
    return jnp.where((source == partner) & (target < HD), 1.0, 0.0).astype(jnp.bfloat16)


def row_tools(rows_ref, at, cos, sin, swap):
    lane = lane_iota((PACK_ROWS, LANES))

    def tile(t):
        return rows_ref[at, t * LANES : (t + 1) * LANES]

    def granules(base, count, target):
        t, g = base // LANES, base % LANES
        value = turned(tile(t), target - g)
        if g + 32 * count > LANES:
            cut = target + LANES - g
            value = jnp.where(lane < cut, value, turned(tile(t + 1), target - g))
        return value

    def rope(base):
        x = granules(base, 3, 0)
        other = jnp.dot(x, swap, preferred_element_type=jnp.float32)
        return (x.astype(jnp.float32) * cos + other * sin).astype(jnp.bfloat16)

    return lane, granules, rope


def pack_kernel(
    x_ref, seg_ref, widths_ref, kv_ref, q_ref, cos_ref, sin_ref, code_ref, rows_ref, ids_ref, wide_ref, row_sems, sems
):
    base, ids_copy = id_window(seg_ref, ids_ref, sems.at[0])
    widths_copy = pltpu.make_async_copy(widths_ref, wide_ref, sems.at[1])
    ids_copy.start()
    widths_copy.start()
    copies = row_copies(x_ref, rows_ref, row_sems)
    for copy in copies:
        copy.start()
    first_tok = device_index() * OWN
    rows = lax.broadcasted_iota(jnp.int32, (OWN, 1), 0)
    lanes = lane_iota((1, LANES))
    freq = jnp.zeros((1, LANES), jnp.float32)
    quarter = HD // 4
    for j in range(quarter):
        freq = jnp.where(lanes % quarter == j, float(np.float32(10000.0 ** (-j / quarter))), freq)
    swap = swap_matrix()
    ids_copy.wait()
    widths_copy.wait()
    own = jnp.zeros((OWN, LANES), jnp.float32)
    window = [(ids_ref[r : r + 1, :].astype(jnp.float32), (base + r) * LANES + lanes - first_tok) for r in range(SEG_WINDOW)]
    for ids, place in window:
        own = own + jnp.where(place == rows, ids, 0.0)
    own = jnp.sum(own, axis=1, keepdims=True)
    before = jnp.zeros((OWN, LANES), jnp.float32)
    for ids, place in window:
        before = before + jnp.where((ids == own) & (place < rows), 1.0, 0.0)
    offset = jnp.sum(before, axis=1, keepdims=True)
    samples = lane_iota((1, SAMPLES)).astype(jnp.float32)
    width = jnp.sum(jnp.where(own == samples, wide_ref[...].astype(jnp.float32), 0.0), axis=1, keepdims=True)
    row_pos = jnp.floor((offset + 0.5) / width)
    col_pos = offset - row_pos * width
    angle = jnp.where(lanes < HD // 2, row_pos, col_pos) * freq
    sine = jnp.sin(angle)
    cos_ref[...] = jnp.cos(angle)
    sin_ref[...] = jnp.where((lanes % (HD // 2)) < quarter, -sine, sine)
    ids = own.astype(jnp.int32)
    shift = jnp.clip(jnp.where(lanes < CODE + BITS, lanes - CODE, lanes - CODE - BITS), 0, BITS - 1)
    bit = (ids >> shift) & 1
    code = jnp.where(lanes < CODE + BITS, 1 - bit, bit)
    code = jnp.where(lanes == ONE, 1, jnp.where((lanes >= CODE) & (lanes < ONE), code, 0))
    code_ref[...] = code.astype(jnp.float32).astype(jnp.bfloat16)
    for copy in copies:
        copy.wait()

    def step(i, carry):
        at = pl.ds(pl.multiple_of(i * PACK_ROWS, PACK_ROWS), PACK_ROWS)
        lane, granules, rope = row_tools(rows_ref, at, cos_ref[at, :], sin_ref[at, :], swap)
        for z in range(GROUP):
            q0 = z * 3 * HD
            k0, v0 = D + q0, 2 * D + q0
            for h in range(3):
                kv_ref[z, at, h * LANES : (h + 1) * LANES] = jnp.where(
                    lane < HD, rope(k0 + h * HD), granules(v0 + 32 * h, 1, HD)
                )
            kv_ref[z, at, 3 * LANES : 4 * LANES] = jnp.where(
                lane < HD, granules(v0 + HD, 3, 0), granules(v0 + 2 * HD, 1, HD)
            )
            q2 = rope(q0 + 2 * HD)
            tail = jnp.where(lane < HD, code_ref[at, :], turned(q2, 32))
            kv_ref[z, at, 4 * LANES : 5 * LANES] = jnp.where(lane < CODE, granules(v0 + 2 * HD + 32, 2, 0), tail)
            q_ref[z, at, :LANES] = jnp.where(lane < HD, rope(q0), turned(q2, HD))
            q_ref[z, at, LANES:] = jnp.where(lane < HD, rope(q0 + HD), turned(q2, 64))
        return carry

    lax.fori_loop(0, OWN // PACK_ROWS, step, 0)


def pack(projected, seg_rows, widths_row):
    vmem, hbm = pl.BlockSpec(memory_space=pltpu.VMEM), pl.BlockSpec(memory_space=pltpu.HBM)
    return pl.pallas_call(
        pack_kernel,
        out_shape=[
            jax.ShapeDtypeStruct((GROUP, OWN, KV_LANES), jnp.bfloat16),
            jax.ShapeDtypeStruct((GROUP, OWN, Q_LANES), jnp.bfloat16),
        ],
        in_specs=[hbm] * 3,
        out_specs=[vmem] * 2,
        scratch_shapes=[
            pltpu.VMEM((OWN, LANES), jnp.float32),
            pltpu.VMEM((OWN, LANES), jnp.float32),
            pltpu.VMEM((OWN, LANES), jnp.bfloat16),
            pltpu.VMEM((OWN, 3 * D), jnp.bfloat16),
            pltpu.VMEM((SEG_WINDOW, LANES), jnp.int32),
            pltpu.VMEM((1, SAMPLES), jnp.int32),
            pltpu.SemaphoreType.DMA((OWN // PACK_ROWS,)),
            pltpu.SemaphoreType.DMA((2,)),
        ],
        compiler_params=pltpu.CompilerParams(vmem_limit_bytes=10 * 1024 * 1024),
        name="pack",
    )(projected, seg_rows, widths_row)


def key_ranges(seg_ref, start_ref, count_ref):
    shard = lax.axis_index("seq")

    def ids_of(index):
        return seg_ref[pl.ds(pl.multiple_of(index * SHARD_ROWS, 4), SHARD_ROWS), :].astype(jnp.float32)

    own_ids = ids_of(shard)
    prev_ids = jnp.where(shard > 0, ids_of(jnp.maximum(shard - 1, 0)), -1.0)
    next_ids = jnp.where(shard < SEQ - 1, ids_of(jnp.minimum(shard + 1, SEQ - 1)), -1.0)
    place = lax.broadcasted_iota(jnp.int32, (SHARD_ROWS, LANES), 0) * LANES + lane_iota((SHARD_ROWS, LANES))

    def total(x):
        return jnp.sum(jnp.sum(x, axis=0, keepdims=True), axis=1, keepdims=True)

    begin, end = WINDOW, 0
    for b in range(BLOCKS):
        first = total(jnp.where(place == b * BQ, own_ids, 0.0))
        last = total(jnp.where(place == b * BQ + BQ - 1, own_ids, 0.0))
        low = total(jnp.where(own_ids < first, 1.0, 0.0) - jnp.where(prev_ids == first, 1.0, 0.0))
        high = total(jnp.where(own_ids <= last, 1.0, 0.0) + jnp.where(next_ids == last, 1.0, 0.0))
        lo, hi = low[0, 0].astype(jnp.int32) + SHARD, high[0, 0].astype(jnp.int32) + SHARD
        start = lo // LANES * LANES
        count = (hi - start + BK - 1) // BK
        start = jnp.minimum(start, WINDOW - count * BK)
        start_ref[b] = start
        count_ref[b] = count
        begin = jnp.minimum(begin, start)
        end = jnp.maximum(end, start + count * BK)
    return begin, end


def gather_keys(prev_ref, own_ref, next_ref, seg_ref, kv_ref, v0_ref, start_ref, count_ref):
    begin, end = key_ranges(seg_ref, start_ref, count_ref)
    first_chunk, last_chunk = begin // CHUNK, (end + CHUNK - 1) // CHUNK
    shard_chunks = SHARD // CHUNK

    def copy_from(ref, number):
        low, high = number * shard_chunks, (number + 1) * shard_chunks

        def move(i, carry):
            src = pl.ds(pl.multiple_of((i - low) * CHUNK, CHUNK), CHUNK)
            dst = pl.ds(pl.multiple_of(i * CHUNK, CHUNK), CHUNK)
            lane = lane_iota((CHUNK, LANES))
            parts = []
            for t in range(5):
                value = ref[src, t * LANES : (t + 1) * LANES]
                kv_ref[dst, t * LANES : (t + 1) * LANES] = value
                parts.append(value)
            v0 = jnp.where(lane < 32, turned(parts[0], 32), jnp.where(lane < 64, turned(parts[1], 64), turned(parts[2], 96)))
            v0_ref[dst, :] = jnp.where(lane < HD, v0, jnp.where(lane == HD, 1.0, 0.0).astype(jnp.bfloat16))
            return carry

        lax.fori_loop(jnp.clip(first_chunk, low, high), jnp.clip(last_chunk, low, high), move, 0)

    copy_from(prev_ref, 0)
    copy_from(own_ref, 1)
    copy_from(next_ref, 2)


def attend_kernel(
    prev_ref, own_ref, next_ref, q_ref, seg_ref, out_ref, kv_ref, v0_ref, qa_ref, qc_ref,
    s0_ref, s1_ref, s2_ref, m0_ref, m1_ref, m2_ref, o0_ref, o1_ref, o2_ref, start_ref, count_ref,
):
    gather_keys(prev_ref, own_ref, next_ref, seg_ref, kv_ref, v0_ref, start_ref, count_ref)
    s_refs, m_refs, o_refs = (s0_ref, s1_ref, s2_ref), (m0_ref, m1_ref, m2_ref), (o0_ref, o1_ref, o2_ref)

    def arrange(b, carry):
        at = pl.ds(pl.multiple_of(b * BQ, BQ), BQ)
        lane = lane_iota((BQ, LANES))
        zero = jnp.zeros((BQ, LANES), jnp.bfloat16)
        t4 = own_ref[at, 4 * LANES :]
        t5 = q_ref[at, :LANES]
        t6 = q_ref[at, LANES:]
        qa_ref[0, at, :] = jnp.where(lane < HD, t5, zero)
        qa_ref[1, at, :] = jnp.where(lane < HD, t6, zero)
        q2 = jnp.where(lane < 32, turned(t5, 32), jnp.where(lane < 64, turned(t6, 64), turned(t4, 96)))
        qa_ref[2, at, :] = jnp.where(lane < HD, q2, zero)
        other = (t4.astype(jnp.float32) - 1.0) * BIG
        qc_ref[at, :] = jnp.where((lane >= CODE) & (lane < ONE), other, 0.0).astype(jnp.bfloat16)
        return carry

    lax.fori_loop(0, BLOCKS, arrange, 0)

    def block(b, carry):
        start, count = start_ref[b], count_ref[b]
        at = pl.ds(pl.multiple_of(b * BQ, BQ), BQ)
        for ref in m_refs:
            ref[...] = jnp.full_like(ref, -3.0e38)
        for ref in o_refs:
            ref[...] = jnp.zeros_like(ref)

        def keys_of(j):
            return pl.ds(pl.multiple_of(start + j * BK, LANES), BK)

        def scores(h, j):
            keys = keys_of(j)
            k = jnp.concatenate([kv_ref[keys, h * LANES : (h + 1) * LANES], kv_ref[keys, 4 * LANES :]], axis=1)
            q = jnp.concatenate([qa_ref[h, at, :], qc_ref[at, :]], axis=1)
            s = lax.dot_general(q, k, (((1,), (1,)), ((), ())), preferred_element_type=jnp.float32)
            s_refs[h][j] = s
            top = s[:, :LANES]
            for t in range(1, BK // LANES):
                top = jnp.maximum(top, s[:, t * LANES : (t + 1) * LANES])
            m_refs[h][...] = jnp.maximum(m_refs[h][...], top)

        def blend(h, j):
            keys = keys_of(j)
            m = jnp.concatenate([m_refs[h][...]] * (BK // LANES), axis=1)
            weights = jnp.exp2(s_refs[h][j] * SCALE - m).astype(jnp.bfloat16)
            values = v0_ref[keys, :] if h == 0 else kv_ref[keys, 3 * LANES :]
            o_refs[h][...] += jnp.dot(weights, values, preferred_element_type=jnp.float32)

        def first_pass(j, c):
            for h in range(3):
                scores(h, j)
            return c

        def second_pass(j, c):
            for h in range(3):
                blend(h, j)
            return c

        lax.fori_loop(0, count, first_pass, 0)
        for ref in m_refs:
            ref[...] = jnp.broadcast_to(jnp.max(ref[...], axis=1, keepdims=True) * SCALE, (BQ, LANES))
        lax.fori_loop(0, count, second_pass, 0)

        lane = lane_iota((OWN, LANES))
        part = OWN // 4
        part_lane = lane_iota((part, LANES))
        for i in range(BQ // OWN):
            at = slice(i * OWN, (i + 1) * OWN)
            to = b * (BQ // OWN) + i
            o0 = o0_ref[at, :]
            o0 = o0 / o0[:, HD : HD + 1]
            o1 = o1_ref[at, :LANES] / o1_ref[at, LANES:][:, ONE : ONE + 1]
            o2a, o2b = o2_ref[at, :LANES], o2_ref[at, LANES:]
            t2 = o2b[:, ONE : ONE + 1]
            o2a, o2b = o2a / t2, o2b / t2
            out_ref[to, :OWN, :] = jnp.where(lane < HD, o0, o2a).astype(jnp.bfloat16)
            out_ref[to, OWN : 2 * OWN, :] = jnp.where(lane < HD, o1, turned(o2b, 96)).astype(jnp.bfloat16)
            fold = turned(o2b[:part], 96)
            for g in range(1, 4):
                fold = jnp.where(part_lane < 32 * g, fold, turned(o2b[g * part : (g + 1) * part], 32 * g - 32))
            out_ref[to, 2 * OWN :, :] = fold.astype(jnp.bfloat16)
        return carry

    lax.fori_loop(0, BLOCKS, block, 0)


def attend(prev, own, following, queries, seg_rows):
    vmem = pl.BlockSpec(memory_space=pltpu.VMEM)
    return pl.pallas_call(
        attend_kernel,
        out_shape=jax.ShapeDtypeStruct((GROUP, OUT_ROWS, LANES), jnp.bfloat16),
        in_specs=[vmem] * 5,
        out_specs=vmem,
        scratch_shapes=[
            pltpu.VMEM((WINDOW, KV_LANES), jnp.bfloat16),
            pltpu.VMEM((WINDOW, LANES), jnp.bfloat16),
            pltpu.VMEM((3, SHARD, LANES), jnp.bfloat16),
            pltpu.VMEM((SHARD, LANES), jnp.bfloat16),
            *[pltpu.VMEM((MAX_STEPS, BQ, BK), jnp.float32)] * 3,
            *[pltpu.VMEM((BQ, LANES), jnp.float32)] * 4,
            *[pltpu.VMEM((BQ, 2 * LANES), jnp.float32)] * 2,
            pltpu.SMEM((BLOCKS,), jnp.int32),
            pltpu.SMEM((BLOCKS,), jnp.int32),
        ],
        compiler_params=pltpu.CompilerParams(vmem_limit_bytes=40 * 1024 * 1024),
        name="attend",
    )(prev, own, following, queries, seg_rows)


def unpack_kernel(in_ref, out_ref):
    lane = lane_iota((OWN, LANES))
    part = OWN // 4

    def source(z, i):
        if i < 3:
            return in_ref[z, :OWN, :], i
        if i < 6:
            return in_ref[z, OWN : 2 * OWN, :], i - 3
        return in_ref[z, (i - 6) * OWN : (i - 5) * OWN, :], 3

    for t in range(D // LANES):
        value = None
        for g in range(4):
            z, i = divmod(4 * t + g, 9)
            if i == 8:
                pieces = [turned(in_ref[z, 2 * OWN :, :], 32 * (g - p)) for p in range(4)]
                moved = jnp.concatenate(pieces, axis=0)
            else:
                tile, at = source(z, i)
                moved = turned(tile, 32 * (g - at))
            value = moved if value is None else jnp.where(lane < 32 * g, value, moved)
        out_ref[:, t * LANES : (t + 1) * LANES] = value


def unpack(returned):
    vmem = pl.BlockSpec(memory_space=pltpu.VMEM)
    return pl.pallas_call(
        unpack_kernel,
        out_shape=jax.ShapeDtypeStruct((OWN, D), jnp.bfloat16),
        in_specs=[vmem],
        out_specs=vmem,
        compiler_params=pltpu.CompilerParams(vmem_limit_bytes=8 * 1024 * 1024),
        name="unpack",
    )(returned)


def body(projected, segment_ids, widths):
    seg_rows = segment_ids.reshape(SEG_ROWS, LANES)
    in_hbm = [pltpu.with_memory_space_constraint(a, pltpu.HBM) for a in (projected, seg_rows, widths.reshape(1, SAMPLES))]
    kv, q = pack(*in_hbm)
    kv = lax.all_to_all(kv, "head", 0, 0, tiled=True)
    kv, q = lax.optimization_barrier((kv, q))
    own = kv.reshape(SHARD, KV_LANES)
    up = [(i, (i + 1) % SEQ) for i in range(SEQ)]
    down = [(j, i) for i, j in up]
    prev = lax.ppermute(own, "seq", up)
    following = lax.ppermute(own, "seq", down)
    q = lax.all_to_all(q, "head", 0, 0, tiled=True)
    out = attend(prev, own, following, q.reshape(SHARD, Q_LANES), seg_rows)
    out = lax.all_to_all(out, "head", 0, 0, tiled=True)
    return unpack(out)


def solution(mesh):
    in_specs = (P(("seq", "head"), None), P(), P())
    out_specs = P(("seq", "head"), None)
    return jax.shard_map(body, mesh=mesh, in_specs=in_specs, out_specs=out_specs, check_vma=False)
```

```python
import math

import jax
import jax.numpy as jnp
import numpy as np
from jax import lax
from jax.experimental import pallas as pl
from jax.experimental.pallas import tpu as pltpu
from jax.sharding import PartitionSpec as P

D = 2304
HEADS = 24
HD = 96
TOKENS = 49152
SAMPLES = 64
GROUP = 8
SEQ = 32
OWN = 192
SHARD = OWN * GROUP
LANES = 128
SEG_ROWS = TOKENS // LANES
SHARD_ROWS = SHARD // LANES

KV_LANES = 5 * LANES
Q_LANES = 2 * LANES
CODE = 64
BITS = 6
ONE = CODE + 2 * BITS
BIG = float(2**20)
BQ = 2 * OWN
BLOCKS = SHARD // BQ
BK = 768
BT = 256
MAX_LONG = 4
MAX_SHORT = 3
CHUNK = 256
PACK_ROWS = 64
SEG_WINDOW = 24
WINDOW = 3 * SHARD
OUT_ROWS = 2 * OWN + OWN // 4
SCALE = math.log2(math.e) / math.sqrt(HD)


def lane_iota(shape, dtype=jnp.int32):
    return lax.broadcasted_iota(dtype, shape, len(shape) - 1)


def turned(x, amount):
    amount %= LANES
    return x if amount == 0 else pltpu.roll(x, amount, 1)


def id_window(seg_ref, ids_ref, sem):
    first_row = jnp.maximum(device_index() * OWN // LANES - SHARD_ROWS, 0)
    base = pl.multiple_of(jnp.minimum(first_row // 8 * 8, SEG_ROWS - SEG_WINDOW), 8)
    return base, pltpu.make_async_copy(seg_ref.at[pl.ds(base, SEG_WINDOW), :], ids_ref, sem)


def device_index():
    return lax.axis_index("seq") * GROUP + lax.axis_index("head")


def row_copies(x_ref, rows_ref, sems):
    count = OWN // PACK_ROWS
    parts = [pl.ds(i * PACK_ROWS, PACK_ROWS) for i in range(count)]
    return [pltpu.make_async_copy(x_ref.at[p, :], rows_ref.at[p, :], sems.at[i]) for i, p in enumerate(parts)]


def swap_matrix():
    source = lax.broadcasted_iota(jnp.int32, (LANES, LANES), 0)
    target = lane_iota((LANES, LANES))
    partner = jnp.where((target % (HD // 2)) < HD // 4, target + HD // 4, target - HD // 4)
    return jnp.where((source == partner) & (target < HD), 1.0, 0.0).astype(jnp.bfloat16)


def row_tools(rows_ref, at, cos, sin, swap):
    lane = lane_iota((PACK_ROWS, LANES))

    def tile(t):
        return rows_ref[at, t * LANES : (t + 1) * LANES]

    def granules(base, count, target):
        t, g = base // LANES, base % LANES
        value = turned(tile(t), target - g)
        if g + 32 * count > LANES:
            cut = target + LANES - g
            value = jnp.where(lane < cut, value, turned(tile(t + 1), target - g))
        return value

    def rope(base):
        x = granules(base, 3, 0)
        other = jnp.dot(x, swap, preferred_element_type=jnp.float32)
        return (x.astype(jnp.float32) * cos + other * sin).astype(jnp.bfloat16)

    return lane, granules, rope


def pack_kernel(
    x_ref, seg_ref, widths_ref, kv_ref, q_ref, cos_ref, sin_ref, code_ref, rows_ref, ids_ref, wide_ref, row_sems, sems
):
    base, ids_copy = id_window(seg_ref, ids_ref, sems.at[0])
    widths_copy = pltpu.make_async_copy(widths_ref, wide_ref, sems.at[1])
    ids_copy.start()
    widths_copy.start()
    copies = row_copies(x_ref, rows_ref, row_sems)
    for copy in copies:
        copy.start()
    first_tok = device_index() * OWN
    rows = lax.broadcasted_iota(jnp.int32, (OWN, 1), 0)
    lanes = lane_iota((1, LANES))
    freq = jnp.zeros((1, LANES), jnp.float32)
    quarter = HD // 4
    for j in range(quarter):
        freq = jnp.where(lanes % quarter == j, float(np.float32(10000.0 ** (-j / quarter))), freq)
    swap = swap_matrix()
    ids_copy.wait()
    widths_copy.wait()
    own = jnp.zeros((OWN, LANES), jnp.float32)
    window = [(ids_ref[r : r + 1, :].astype(jnp.float32), (base + r) * LANES + lanes - first_tok) for r in range(SEG_WINDOW)]
    for ids, place in window:
        own = own + jnp.where(place == rows, ids, 0.0)
    own = jnp.sum(own, axis=1, keepdims=True)
    before = jnp.zeros((OWN, LANES), jnp.float32)
    for ids, place in window:
        before = before + jnp.where((ids == own) & (place < rows), 1.0, 0.0)
    offset = jnp.sum(before, axis=1, keepdims=True)
    samples = lane_iota((1, SAMPLES)).astype(jnp.float32)
    width = jnp.sum(jnp.where(own == samples, wide_ref[...].astype(jnp.float32), 0.0), axis=1, keepdims=True)
    row_pos = jnp.floor((offset + 0.5) / width)
    col_pos = offset - row_pos * width
    angle = jnp.where(lanes < HD // 2, row_pos, col_pos) * freq
    sine = jnp.sin(angle)
    cos_ref[...] = jnp.cos(angle)
    sin_ref[...] = jnp.where((lanes % (HD // 2)) < quarter, -sine, sine)
    ids = own.astype(jnp.int32)
    shift = jnp.clip(jnp.where(lanes < CODE + BITS, lanes - CODE, lanes - CODE - BITS), 0, BITS - 1)
    bit = (ids >> shift) & 1
    code = jnp.where(lanes < CODE + BITS, 1 - bit, bit)
    code = jnp.where(lanes == ONE, 1, jnp.where((lanes >= CODE) & (lanes < ONE), code, 0))
    code_ref[...] = code.astype(jnp.float32).astype(jnp.bfloat16)
    for copy in copies:
        copy.wait()

    def step(i, carry):
        at = pl.ds(pl.multiple_of(i * PACK_ROWS, PACK_ROWS), PACK_ROWS)
        lane, granules, rope = row_tools(rows_ref, at, cos_ref[at, :], sin_ref[at, :], swap)
        for z in range(GROUP):
            q0 = z * 3 * HD
            k0, v0 = D + q0, 2 * D + q0
            for h in range(3):
                kv_ref[z, at, h * LANES : (h + 1) * LANES] = jnp.where(
                    lane < HD, rope(k0 + h * HD), granules(v0 + 32 * h, 1, HD)
                )
            kv_ref[z, at, 3 * LANES : 4 * LANES] = jnp.where(
                lane < HD, granules(v0 + HD, 3, 0), granules(v0 + 2 * HD, 1, HD)
            )
            q2 = rope(q0 + 2 * HD)
            tail = jnp.where(lane < HD, code_ref[at, :], turned(q2, 32))
            kv_ref[z, at, 4 * LANES : 5 * LANES] = jnp.where(lane < CODE, granules(v0 + 2 * HD + 32, 2, 0), tail)
            q_ref[z, at, :LANES] = jnp.where(lane < HD, rope(q0), turned(q2, HD))
            q_ref[z, at, LANES:] = jnp.where(lane < HD, rope(q0 + HD), turned(q2, 64))
        return carry

    lax.fori_loop(0, OWN // PACK_ROWS, step, 0)


def pack(projected, seg_rows, widths_row):
    vmem, hbm = pl.BlockSpec(memory_space=pltpu.VMEM), pl.BlockSpec(memory_space=pltpu.HBM)
    return pl.pallas_call(
        pack_kernel,
        out_shape=[
            jax.ShapeDtypeStruct((GROUP, OWN, KV_LANES), jnp.bfloat16),
            jax.ShapeDtypeStruct((GROUP, OWN, Q_LANES), jnp.bfloat16),
        ],
        in_specs=[hbm] * 3,
        out_specs=[vmem] * 2,
        scratch_shapes=[
            pltpu.VMEM((OWN, LANES), jnp.float32),
            pltpu.VMEM((OWN, LANES), jnp.float32),
            pltpu.VMEM((OWN, LANES), jnp.bfloat16),
            pltpu.VMEM((OWN, 3 * D), jnp.bfloat16),
            pltpu.VMEM((SEG_WINDOW, LANES), jnp.int32),
            pltpu.VMEM((1, SAMPLES), jnp.int32),
            pltpu.SemaphoreType.DMA((OWN // PACK_ROWS,)),
            pltpu.SemaphoreType.DMA((2,)),
        ],
        compiler_params=pltpu.CompilerParams(vmem_limit_bytes=10 * 1024 * 1024),
        name="pack",
    )(projected, seg_rows, widths_row)


def key_ranges(seg_ref, start_ref, count_ref):
    shard = lax.axis_index("seq")

    def ids_of(index):
        return seg_ref[pl.ds(pl.multiple_of(index * SHARD_ROWS, 4), SHARD_ROWS), :].astype(jnp.float32)

    own_ids = ids_of(shard)
    prev_ids = jnp.where(shard > 0, ids_of(jnp.maximum(shard - 1, 0)), -1.0)
    next_ids = jnp.where(shard < SEQ - 1, ids_of(jnp.minimum(shard + 1, SEQ - 1)), -1.0)
    place = lax.broadcasted_iota(jnp.int32, (SHARD_ROWS, LANES), 0) * LANES + lane_iota((SHARD_ROWS, LANES))

    def total(x):
        return jnp.sum(jnp.sum(x, axis=0, keepdims=True), axis=1, keepdims=True)

    begin, end = WINDOW, 0
    for b in range(BLOCKS):
        first = total(jnp.where(place == b * BQ, own_ids, 0.0))
        last = total(jnp.where(place == b * BQ + BQ - 1, own_ids, 0.0))
        low = total(jnp.where(own_ids < first, 1.0, 0.0) - jnp.where(prev_ids == first, 1.0, 0.0))
        high = total(jnp.where(own_ids <= last, 1.0, 0.0) + jnp.where(next_ids == last, 1.0, 0.0))
        lo, hi = low[0, 0].astype(jnp.int32) + SHARD, high[0, 0].astype(jnp.int32) + SHARD
        start = lo // LANES * LANES
        count = (hi - start + BT - 1) // BT
        start = jnp.minimum(start, WINDOW - count * BT)
        start_ref[b] = start
        count_ref[b] = count
        begin = jnp.minimum(begin, start)
        end = jnp.maximum(end, start + count * BT)
    return begin, end


def gather_keys(prev_ref, own_ref, next_ref, seg_ref, kv_ref, v0_ref, start_ref, count_ref):
    begin, end = key_ranges(seg_ref, start_ref, count_ref)
    first_chunk, last_chunk = begin // CHUNK, (end + CHUNK - 1) // CHUNK
    shard_chunks = SHARD // CHUNK

    def copy_from(ref, number):
        low, high = number * shard_chunks, (number + 1) * shard_chunks

        def move(i, carry):
            src = pl.ds(pl.multiple_of((i - low) * CHUNK, CHUNK), CHUNK)
            dst = pl.ds(pl.multiple_of(i * CHUNK, CHUNK), CHUNK)
            lane = lane_iota((CHUNK, LANES))
            parts = []
            for t in range(5):
                value = ref[src, t * LANES : (t + 1) * LANES]
                kv_ref[dst, t * LANES : (t + 1) * LANES] = value
                parts.append(value)
            v0 = jnp.where(lane < 32, turned(parts[0], 32), jnp.where(lane < 64, turned(parts[1], 64), turned(parts[2], 96)))
            v0_ref[dst, :] = jnp.where(lane < HD, v0, jnp.where(lane == HD, 1.0, 0.0).astype(jnp.bfloat16))
            return carry

        lax.fori_loop(jnp.clip(first_chunk, low, high), jnp.clip(last_chunk, low, high), move, 0)

    copy_from(prev_ref, 0)
    copy_from(own_ref, 1)
    copy_from(next_ref, 2)


def attend_kernel(
    prev_ref, own_ref, next_ref, q_ref, seg_ref, out_ref, kv_ref, v0_ref, qa_ref, qc_ref,
    s0_ref, s1_ref, s2_ref, t0_ref, t1_ref, t2_ref, m0_ref, m1_ref, m2_ref, o0_ref, o1_ref, o2_ref, start_ref, count_ref,
):
    gather_keys(prev_ref, own_ref, next_ref, seg_ref, kv_ref, v0_ref, start_ref, count_ref)
    s_refs, t_refs = (s0_ref, s1_ref, s2_ref), (t0_ref, t1_ref, t2_ref)
    m_refs, o_refs = (m0_ref, m1_ref, m2_ref), (o0_ref, o1_ref, o2_ref)

    def arrange(b, carry):
        at = pl.ds(pl.multiple_of(b * BQ, BQ), BQ)
        lane = lane_iota((BQ, LANES))
        zero = jnp.zeros((BQ, LANES), jnp.bfloat16)
        t4 = own_ref[at, 4 * LANES :]
        t5 = q_ref[at, :LANES]
        t6 = q_ref[at, LANES:]
        qa_ref[0, at, :] = jnp.where(lane < HD, t5, zero)
        qa_ref[1, at, :] = jnp.where(lane < HD, t6, zero)
        q2 = jnp.where(lane < 32, turned(t5, 32), jnp.where(lane < 64, turned(t6, 64), turned(t4, 96)))
        qa_ref[2, at, :] = jnp.where(lane < HD, q2, zero)
        other = (t4.astype(jnp.float32) - 1.0) * BIG
        qc_ref[at, :] = jnp.where((lane >= CODE) & (lane < ONE), other, 0.0).astype(jnp.bfloat16)
        return carry

    lax.fori_loop(0, BLOCKS, arrange, 0)

    def block(b, carry):
        start, count = start_ref[b], count_ref[b]
        at = pl.ds(pl.multiple_of(b * BQ, BQ), BQ)
        for ref in m_refs:
            ref[...] = jnp.full_like(ref, -3.0e38)
        for ref in o_refs:
            ref[...] = jnp.zeros_like(ref)

        def scores(first_key, size, s_refs, j):
            keys = pl.ds(pl.multiple_of(first_key + j * size, LANES), size)
            t4 = kv_ref[keys, 4 * LANES :]
            for h in range(3):
                k = jnp.concatenate([kv_ref[keys, h * LANES : (h + 1) * LANES], t4], axis=1)
                q = jnp.concatenate([qa_ref[h, at, :], qc_ref[at, :]], axis=1)
                s = lax.dot_general(q, k, (((1,), (1,)), ((), ())), preferred_element_type=jnp.float32)
                s_refs[h][j] = s
                top = s[:, :LANES]
                for t in range(1, size // LANES):
                    top = jnp.maximum(top, s[:, t * LANES : (t + 1) * LANES])
                m_refs[h][...] = jnp.maximum(m_refs[h][...], top)

        def blend(first_key, size, s_refs, j):
            keys = pl.ds(pl.multiple_of(first_key + j * size, LANES), size)
            for h in range(3):
                m = jnp.concatenate([m_refs[h][...]] * (size // LANES), axis=1)
                weights = jnp.exp2(s_refs[h][j] * SCALE - m).astype(jnp.bfloat16)
                values = v0_ref[keys, :] if h == 0 else kv_ref[keys, 3 * LANES :]
                o_refs[h][...] += jnp.dot(weights, values, preferred_element_type=jnp.float32)

        per_long = BK // BT
        longs = count // per_long
        parts = ((start, BK, s_refs, longs), (start + longs * BK, BT, t_refs, count - longs * per_long))

        def over_keys(what):
            for first_key, size, refs, steps in parts:
                lax.fori_loop(0, steps, lambda j, c: what(first_key, size, refs, j) or c, 0)

        over_keys(scores)
        for ref in m_refs:
            ref[...] = jnp.broadcast_to(jnp.max(ref[...], axis=1, keepdims=True) * SCALE, (BQ, LANES))
        over_keys(blend)

        lane = lane_iota((OWN, LANES))
        part = OWN // 4
        part_lane = lane_iota((part, LANES))
        for i in range(BQ // OWN):
            at = slice(i * OWN, (i + 1) * OWN)
            to = b * (BQ // OWN) + i
            o0 = o0_ref[at, :]
            o0 = o0 * (1.0 / o0[:, HD : HD + 1])
            o1 = o1_ref[at, :LANES] * (1.0 / o1_ref[at, LANES:][:, ONE : ONE + 1])
            o2a, o2b = o2_ref[at, :LANES], o2_ref[at, LANES:]
            r2 = 1.0 / o2b[:, ONE : ONE + 1]
            o2a, o2b = o2a * r2, o2b * r2
            out_ref[to, :OWN, :] = jnp.where(lane < HD, o0, o2a).astype(jnp.bfloat16)
            out_ref[to, OWN : 2 * OWN, :] = jnp.where(lane < HD, o1, turned(o2b, 96)).astype(jnp.bfloat16)
            fold = turned(o2b[:part], 96)
            for g in range(1, 4):
                fold = jnp.where(part_lane < 32 * g, fold, turned(o2b[g * part : (g + 1) * part], 32 * g - 32))
            out_ref[to, 2 * OWN :, :] = fold.astype(jnp.bfloat16)
        return carry

    lax.fori_loop(0, BLOCKS, block, 0)


def attend(prev, own, following, queries, seg_rows):
    vmem = pl.BlockSpec(memory_space=pltpu.VMEM)
    return pl.pallas_call(
        attend_kernel,
        out_shape=jax.ShapeDtypeStruct((GROUP, OUT_ROWS, LANES), jnp.bfloat16),
        in_specs=[vmem] * 5,
        out_specs=vmem,
        scratch_shapes=[
            pltpu.VMEM((WINDOW, KV_LANES), jnp.bfloat16),
            pltpu.VMEM((WINDOW, LANES), jnp.bfloat16),
            pltpu.VMEM((3, SHARD, LANES), jnp.bfloat16),
            pltpu.VMEM((SHARD, LANES), jnp.bfloat16),
            *[pltpu.VMEM((MAX_LONG, BQ, BK), jnp.float32)] * 3,
            *[pltpu.VMEM((MAX_SHORT, BQ, BT), jnp.float32)] * 3,
            *[pltpu.VMEM((BQ, LANES), jnp.float32)] * 4,
            *[pltpu.VMEM((BQ, 2 * LANES), jnp.float32)] * 2,
            pltpu.SMEM((BLOCKS,), jnp.int32),
            pltpu.SMEM((BLOCKS,), jnp.int32),
        ],
        compiler_params=pltpu.CompilerParams(vmem_limit_bytes=40 * 1024 * 1024),
        name="attend",
    )(prev, own, following, queries, seg_rows)


def unpack_kernel(in_ref, out_ref):
    lane = lane_iota((OWN, LANES))
    part = OWN // 4

    def source(z, i):
        if i < 3:
            return in_ref[z, :OWN, :], i
        if i < 6:
            return in_ref[z, OWN : 2 * OWN, :], i - 3
        return in_ref[z, (i - 6) * OWN : (i - 5) * OWN, :], 3

    for t in range(D // LANES):
        value = None
        for g in range(4):
            z, i = divmod(4 * t + g, 9)
            if i == 8:
                pieces = [turned(in_ref[z, 2 * OWN :, :], 32 * (g - p)) for p in range(4)]
                moved = jnp.concatenate(pieces, axis=0)
            else:
                tile, at = source(z, i)
                moved = turned(tile, 32 * (g - at))
            value = moved if value is None else jnp.where(lane < 32 * g, value, moved)
        out_ref[:, t * LANES : (t + 1) * LANES] = value


def unpack(returned):
    vmem = pl.BlockSpec(memory_space=pltpu.VMEM)
    return pl.pallas_call(
        unpack_kernel,
        out_shape=jax.ShapeDtypeStruct((OWN, D), jnp.bfloat16),
        in_specs=[vmem],
        out_specs=vmem,
        compiler_params=pltpu.CompilerParams(vmem_limit_bytes=8 * 1024 * 1024),
        name="unpack",
    )(returned)


def body(projected, segment_ids, widths):
    seg_rows = segment_ids.reshape(SEG_ROWS, LANES)
    in_hbm = [pltpu.with_memory_space_constraint(a, pltpu.HBM) for a in (projected, seg_rows, widths.reshape(1, SAMPLES))]
    kv, q = pack(*in_hbm)
    kv = lax.all_to_all(kv, "head", 0, 0, tiled=True)
    kv, q = lax.optimization_barrier((kv, q))
    own = kv.reshape(SHARD, KV_LANES)
    up = [(i, (i + 1) % SEQ) for i in range(SEQ)]
    down = [(j, i) for i, j in up]
    prev = lax.ppermute(own, "seq", up)
    following = lax.ppermute(own, "seq", down)
    q = lax.all_to_all(q, "head", 0, 0, tiled=True)
    out = attend(prev, own, following, q.reshape(SHARD, Q_LANES), seg_rows)
    out = lax.all_to_all(out, "head", 0, 0, tiled=True)
    return unpack(out)


def solution(mesh):
    in_specs = (P(("seq", "head"), None), P(), P())
    out_specs = P(("seq", "head"), None)
    return jax.shard_map(body, mesh=mesh, in_specs=in_specs, out_specs=out_specs, check_vma=False)
```

```python
import math

import jax
import jax.numpy as jnp
import numpy as np
from jax import lax
from jax.experimental import pallas as pl
from jax.experimental.pallas import tpu as pltpu
from jax.sharding import PartitionSpec as P

D = 2304
HEADS = 24
HD = 96
TOKENS = 49152
SAMPLES = 64
GROUP = 8
SEQ = 32
OWN = 192
SHARD = OWN * GROUP
LANES = 128
SEG_ROWS = TOKENS // LANES
SHARD_ROWS = SHARD // LANES

KV_LANES = 5 * LANES
Q_LANES = 2 * LANES
CODE = 64
BITS = 6
ONE = CODE + 2 * BITS
BIG = float(2**20)
BQ = 2 * OWN
BLOCKS = SHARD // BQ
UNIT = 256
MAX_UNITS = 14
STEPS = (7, 6, 5, 4, 3, 2, 1)
CHUNK = 256
PACK_ROWS = 64
SEG_WINDOW = 24
WINDOW = 3 * SHARD
OUT_ROWS = 2 * OWN + OWN // 4
SCALE = math.log2(math.e) / math.sqrt(HD)


def lane_iota(shape, dtype=jnp.int32):
    return lax.broadcasted_iota(dtype, shape, len(shape) - 1)


def turned(x, amount):
    amount %= LANES
    return x if amount == 0 else pltpu.roll(x, amount, 1)


def id_window(seg_ref, ids_ref, sem):
    first_row = jnp.maximum(device_index() * OWN // LANES - SHARD_ROWS, 0)
    base = pl.multiple_of(jnp.minimum(first_row // 8 * 8, SEG_ROWS - SEG_WINDOW), 8)
    return base, pltpu.make_async_copy(seg_ref.at[pl.ds(base, SEG_WINDOW), :], ids_ref, sem)


def device_index():
    return lax.axis_index("seq") * GROUP + lax.axis_index("head")


def row_copies(x_ref, rows_ref, sems):
    count = OWN // PACK_ROWS
    parts = [pl.ds(i * PACK_ROWS, PACK_ROWS) for i in range(count)]
    return [pltpu.make_async_copy(x_ref.at[p, :], rows_ref.at[p, :], sems.at[i]) for i, p in enumerate(parts)]


def swap_matrix():
    source = lax.broadcasted_iota(jnp.int32, (LANES, LANES), 0)
    target = lane_iota((LANES, LANES))
    partner = jnp.where((target % (HD // 2)) < HD // 4, target + HD // 4, target - HD // 4)
    return jnp.where((source == partner) & (target < HD), 1.0, 0.0).astype(jnp.bfloat16)


def row_tools(rows_ref, at, cos, sin, swap):
    lane = lane_iota((PACK_ROWS, LANES))

    def tile(t):
        return rows_ref[at, t * LANES : (t + 1) * LANES]

    def granules(base, count, target):
        t, g = base // LANES, base % LANES
        value = turned(tile(t), target - g)
        if g + 32 * count > LANES:
            cut = target + LANES - g
            value = jnp.where(lane < cut, value, turned(tile(t + 1), target - g))
        return value

    def rope(base):
        x = granules(base, 3, 0)
        other = jnp.dot(x, swap, preferred_element_type=jnp.float32)
        return (x.astype(jnp.float32) * cos + other * sin).astype(jnp.bfloat16)

    return lane, granules, rope


def pack_kernel(
    x_ref, seg_ref, widths_ref, kv_ref, q_ref, cos_ref, sin_ref, code_ref, rows_ref, ids_ref, wide_ref, row_sems, sems
):
    base, ids_copy = id_window(seg_ref, ids_ref, sems.at[0])
    widths_copy = pltpu.make_async_copy(widths_ref, wide_ref, sems.at[1])
    ids_copy.start()
    widths_copy.start()
    copies = row_copies(x_ref, rows_ref, row_sems)
    for copy in copies:
        copy.start()
    first_tok = device_index() * OWN
    rows = lax.broadcasted_iota(jnp.int32, (OWN, 1), 0)
    lanes = lane_iota((1, LANES))
    freq = jnp.zeros((1, LANES), jnp.float32)
    quarter = HD // 4
    for j in range(quarter):
        freq = jnp.where(lanes % quarter == j, float(np.float32(10000.0 ** (-j / quarter))), freq)
    swap = swap_matrix()
    ids_copy.wait()
    widths_copy.wait()
    own = jnp.zeros((OWN, LANES), jnp.float32)
    window = [(ids_ref[r : r + 1, :].astype(jnp.float32), (base + r) * LANES + lanes - first_tok) for r in range(SEG_WINDOW)]
    for ids, place in window:
        own = own + jnp.where(place == rows, ids, 0.0)
    own = jnp.sum(own, axis=1, keepdims=True)
    before = jnp.zeros((OWN, LANES), jnp.float32)
    for ids, place in window:
        before = before + jnp.where((ids == own) & (place < rows), 1.0, 0.0)
    offset = jnp.sum(before, axis=1, keepdims=True)
    samples = lane_iota((1, SAMPLES)).astype(jnp.float32)
    width = jnp.sum(jnp.where(own == samples, wide_ref[...].astype(jnp.float32), 0.0), axis=1, keepdims=True)
    row_pos = jnp.floor((offset + 0.5) / width)
    col_pos = offset - row_pos * width
    angle = jnp.where(lanes < HD // 2, row_pos, col_pos) * freq
    sine = jnp.sin(angle)
    cos_ref[...] = jnp.cos(angle)
    sin_ref[...] = jnp.where((lanes % (HD // 2)) < quarter, -sine, sine)
    ids = own.astype(jnp.int32)
    shift = jnp.clip(jnp.where(lanes < CODE + BITS, lanes - CODE, lanes - CODE - BITS), 0, BITS - 1)
    bit = (ids >> shift) & 1
    code = jnp.where(lanes < CODE + BITS, 1 - bit, bit)
    code = jnp.where(lanes == ONE, 1, jnp.where((lanes >= CODE) & (lanes < ONE), code, 0))
    code_ref[...] = code.astype(jnp.float32).astype(jnp.bfloat16)
    for copy in copies:
        copy.wait()

    def step(i, carry):
        at = pl.ds(pl.multiple_of(i * PACK_ROWS, PACK_ROWS), PACK_ROWS)
        lane, granules, rope = row_tools(rows_ref, at, cos_ref[at, :], sin_ref[at, :], swap)
        for z in range(GROUP):
            q0 = z * 3 * HD
            k0, v0 = D + q0, 2 * D + q0
            for h in range(3):
                kv_ref[z, at, h * LANES : (h + 1) * LANES] = jnp.where(
                    lane < HD, rope(k0 + h * HD), granules(v0 + 32 * h, 1, HD)
                )
            kv_ref[z, at, 3 * LANES : 4 * LANES] = jnp.where(
                lane < HD, granules(v0 + HD, 3, 0), granules(v0 + 2 * HD, 1, HD)
            )
            q2 = rope(q0 + 2 * HD)
            tail = jnp.where(lane < HD, code_ref[at, :], turned(q2, 32))
            kv_ref[z, at, 4 * LANES : 5 * LANES] = jnp.where(lane < CODE, granules(v0 + 2 * HD + 32, 2, 0), tail)
            q_ref[z, at, :LANES] = jnp.where(lane < HD, rope(q0), turned(q2, HD))
            q_ref[z, at, LANES:] = jnp.where(lane < HD, rope(q0 + HD), turned(q2, 64))
        return carry

    lax.fori_loop(0, OWN // PACK_ROWS, step, 0)


def pack(projected, seg_rows, widths_row):
    vmem, hbm = pl.BlockSpec(memory_space=pltpu.VMEM), pl.BlockSpec(memory_space=pltpu.HBM)
    return pl.pallas_call(
        pack_kernel,
        out_shape=[
            jax.ShapeDtypeStruct((GROUP, OWN, KV_LANES), jnp.bfloat16),
            jax.ShapeDtypeStruct((GROUP, OWN, Q_LANES), jnp.bfloat16),
        ],
        in_specs=[hbm] * 3,
        out_specs=[vmem] * 2,
        scratch_shapes=[
            pltpu.VMEM((OWN, LANES), jnp.float32),
            pltpu.VMEM((OWN, LANES), jnp.float32),
            pltpu.VMEM((OWN, LANES), jnp.bfloat16),
            pltpu.VMEM((OWN, 3 * D), jnp.bfloat16),
            pltpu.VMEM((SEG_WINDOW, LANES), jnp.int32),
            pltpu.VMEM((1, SAMPLES), jnp.int32),
            pltpu.SemaphoreType.DMA((OWN // PACK_ROWS,)),
            pltpu.SemaphoreType.DMA((2,)),
        ],
        compiler_params=pltpu.CompilerParams(vmem_limit_bytes=10 * 1024 * 1024),
        name="pack",
    )(projected, seg_rows, widths_row)


def key_ranges(seg_ref, start_ref, count_ref):
    shard = lax.axis_index("seq")

    def ids_of(index):
        return seg_ref[pl.ds(pl.multiple_of(index * SHARD_ROWS, 4), SHARD_ROWS), :].astype(jnp.float32)

    own_ids = ids_of(shard)
    prev_ids = jnp.where(shard > 0, ids_of(jnp.maximum(shard - 1, 0)), -1.0)
    next_ids = jnp.where(shard < SEQ - 1, ids_of(jnp.minimum(shard + 1, SEQ - 1)), -1.0)
    place = lax.broadcasted_iota(jnp.int32, (SHARD_ROWS, LANES), 0) * LANES + lane_iota((SHARD_ROWS, LANES))

    def total(x):
        return jnp.sum(jnp.sum(x, axis=0, keepdims=True), axis=1, keepdims=True)

    begin, end = WINDOW, 0
    for b in range(BLOCKS):
        first = total(jnp.where(place == b * BQ, own_ids, 0.0))
        last = total(jnp.where(place == b * BQ + BQ - 1, own_ids, 0.0))
        low = total(jnp.where(own_ids < first, 1.0, 0.0) - jnp.where(prev_ids == first, 1.0, 0.0))
        high = total(jnp.where(own_ids <= last, 1.0, 0.0) + jnp.where(next_ids == last, 1.0, 0.0))
        lo, hi = low[0, 0].astype(jnp.int32) + SHARD, high[0, 0].astype(jnp.int32) + SHARD
        start = lo // LANES * LANES
        count = (hi - start + UNIT - 1) // UNIT
        start = jnp.minimum(start, WINDOW - count * UNIT)
        start_ref[b] = start
        count_ref[b] = count
        begin = jnp.minimum(begin, start)
        end = jnp.maximum(end, start + count * UNIT)
    return begin, end


def gather_keys(prev_ref, own_ref, next_ref, seg_ref, kv_ref, v0_ref, start_ref, count_ref):
    begin, end = key_ranges(seg_ref, start_ref, count_ref)
    first_chunk, last_chunk = begin // CHUNK, (end + CHUNK - 1) // CHUNK
    shard_chunks = SHARD // CHUNK

    def copy_from(ref, number):
        low, high = number * shard_chunks, (number + 1) * shard_chunks

        def move(i, carry):
            src = pl.ds(pl.multiple_of((i - low) * CHUNK, CHUNK), CHUNK)
            dst = pl.ds(pl.multiple_of(i * CHUNK, CHUNK), CHUNK)
            lane = lane_iota((CHUNK, LANES))
            parts = []
            for t in range(5):
                value = ref[src, t * LANES : (t + 1) * LANES]
                kv_ref[dst, t * LANES : (t + 1) * LANES] = value
                parts.append(value)
            v0 = jnp.where(lane < 32, turned(parts[0], 32), jnp.where(lane < 64, turned(parts[1], 64), turned(parts[2], 96)))
            v0_ref[dst, :] = jnp.where(lane < HD, v0, jnp.where(lane == HD, 1.0, 0.0).astype(jnp.bfloat16))
            return carry

        lax.fori_loop(jnp.clip(first_chunk, low, high), jnp.clip(last_chunk, low, high), move, 0)

    copy_from(prev_ref, 0)
    copy_from(own_ref, 1)
    copy_from(next_ref, 2)


def attend_kernel(
    prev_ref, own_ref, next_ref, q_ref, seg_ref, out_ref, kv_ref, v0_ref, qa_ref, qc_ref, start_ref, count_ref, *work
):
    gather_keys(prev_ref, own_ref, next_ref, seg_ref, kv_ref, v0_ref, start_ref, count_ref)
    m_refs, o_refs, s_refs = work[:3], work[3:6], work[6:]
    o0_ref, o1_ref, o2_ref = o_refs

    def arrange(b, carry):
        at = pl.ds(pl.multiple_of(b * BQ, BQ), BQ)
        lane = lane_iota((BQ, LANES))
        zero = jnp.zeros((BQ, LANES), jnp.bfloat16)
        t4 = own_ref[at, 4 * LANES :]
        t5 = q_ref[at, :LANES]
        t6 = q_ref[at, LANES:]
        qa_ref[0, at, :] = jnp.where(lane < HD, t5, zero)
        qa_ref[1, at, :] = jnp.where(lane < HD, t6, zero)
        q2 = jnp.where(lane < 32, turned(t5, 32), jnp.where(lane < 64, turned(t6, 64), turned(t4, 96)))
        qa_ref[2, at, :] = jnp.where(lane < HD, q2, zero)
        other = (t4.astype(jnp.float32) - 1.0) * BIG
        qc_ref[at, :] = jnp.where((lane >= CODE) & (lane < ONE), other, 0.0).astype(jnp.bfloat16)
        return carry

    lax.fori_loop(0, BLOCKS, arrange, 0)

    def block(b, carry):
        start, count = start_ref[b], count_ref[b]
        at = pl.ds(pl.multiple_of(b * BQ, BQ), BQ)
        for ref in m_refs:
            ref[...] = jnp.full_like(ref, -3.0e38)
        for ref in o_refs:
            ref[...] = jnp.zeros_like(ref)

        def scores(first_unit, size, j):
            keys = pl.ds(pl.multiple_of(start + first_unit * UNIT + j * size, LANES), size)
            t4 = kv_ref[keys, 4 * LANES :]
            for h in range(3):
                k = jnp.concatenate([kv_ref[keys, h * LANES : (h + 1) * LANES], t4], axis=1)
                q = jnp.concatenate([qa_ref[h, at, :], qc_ref[at, :]], axis=1)
                s = lax.dot_general(q, k, (((1,), (1,)), ((), ())), preferred_element_type=jnp.float32)
                for u in range(size // UNIT):
                    s_refs[h][first_unit + j * (size // UNIT) + u] = s[:, u * UNIT : (u + 1) * UNIT]
                top = s[:, :LANES]
                for t in range(1, size // LANES):
                    top = jnp.maximum(top, s[:, t * LANES : (t + 1) * LANES])
                m_refs[h][...] = jnp.maximum(m_refs[h][...], top)

        def blend(first_unit, size, j):
            keys = pl.ds(pl.multiple_of(start + first_unit * UNIT + j * size, LANES), size)
            for h in range(3):
                m = jnp.concatenate([m_refs[h][...]] * (UNIT // LANES), axis=1)
                weights = jnp.concatenate(
                    [
                        jnp.exp2(s_refs[h][first_unit + j * (size // UNIT) + u] * SCALE - m).astype(jnp.bfloat16)
                        for u in range(size // UNIT)
                    ],
                    axis=1,
                )
                values = v0_ref[keys, :] if h == 0 else kv_ref[keys, 3 * LANES :]
                o_refs[h][...] += jnp.dot(weights, values, preferred_element_type=jnp.float32)

        def over_keys(what):
            done = 0
            for units in STEPS:
                steps = (count - done) // units
                lax.fori_loop(0, steps, lambda j, c: what(done, units * UNIT, j) or c, 0)
                done = done + steps * units

        over_keys(scores)
        for ref in m_refs:
            ref[...] = jnp.broadcast_to(jnp.max(ref[...], axis=1, keepdims=True) * SCALE, (BQ, LANES))
        over_keys(blend)

        lane = lane_iota((OWN, LANES))
        part = OWN // 4
        part_lane = lane_iota((part, LANES))
        for i in range(BQ // OWN):
            at = slice(i * OWN, (i + 1) * OWN)
            to = b * (BQ // OWN) + i
            o0 = o0_ref[at, :]
            o0 = o0 * (1.0 / o0[:, HD : HD + 1])
            o1 = o1_ref[at, :LANES] * (1.0 / o1_ref[at, LANES:][:, ONE : ONE + 1])
            o2a, o2b = o2_ref[at, :LANES], o2_ref[at, LANES:]
            r2 = 1.0 / o2b[:, ONE : ONE + 1]
            o2a, o2b = o2a * r2, o2b * r2
            out_ref[to, :OWN, :] = jnp.where(lane < HD, o0, o2a).astype(jnp.bfloat16)
            out_ref[to, OWN : 2 * OWN, :] = jnp.where(lane < HD, o1, turned(o2b, 96)).astype(jnp.bfloat16)
            fold = turned(o2b[:part], 96)
            for g in range(1, 4):
                fold = jnp.where(part_lane < 32 * g, fold, turned(o2b[g * part : (g + 1) * part], 32 * g - 32))
            out_ref[to, 2 * OWN :, :] = fold.astype(jnp.bfloat16)
        return carry

    lax.fori_loop(0, BLOCKS, block, 0)


def attend(prev, own, following, queries, seg_rows):
    vmem = pl.BlockSpec(memory_space=pltpu.VMEM)
    return pl.pallas_call(
        attend_kernel,
        out_shape=jax.ShapeDtypeStruct((GROUP, OUT_ROWS, LANES), jnp.bfloat16),
        in_specs=[vmem] * 5,
        out_specs=vmem,
        scratch_shapes=[
            pltpu.VMEM((WINDOW, KV_LANES), jnp.bfloat16),
            pltpu.VMEM((WINDOW, LANES), jnp.bfloat16),
            pltpu.VMEM((3, SHARD, LANES), jnp.bfloat16),
            pltpu.VMEM((SHARD, LANES), jnp.bfloat16),
            pltpu.SMEM((BLOCKS,), jnp.int32),
            pltpu.SMEM((BLOCKS,), jnp.int32),
            *[pltpu.VMEM((BQ, LANES), jnp.float32)] * 4,
            *[pltpu.VMEM((BQ, 2 * LANES), jnp.float32)] * 2,
            *[pltpu.VMEM((MAX_UNITS, BQ, UNIT), jnp.float32)] * 3,
        ],
        compiler_params=pltpu.CompilerParams(vmem_limit_bytes=40 * 1024 * 1024),
        name="attend",
    )(prev, own, following, queries, seg_rows)


def unpack_kernel(in_ref, out_ref):
    lane = lane_iota((OWN, LANES))
    part = OWN // 4

    def source(z, i):
        if i < 3:
            return in_ref[z, :OWN, :], i
        if i < 6:
            return in_ref[z, OWN : 2 * OWN, :], i - 3
        return in_ref[z, (i - 6) * OWN : (i - 5) * OWN, :], 3

    for t in range(D // LANES):
        value = None
        for g in range(4):
            z, i = divmod(4 * t + g, 9)
            if i == 8:
                pieces = [turned(in_ref[z, 2 * OWN :, :], 32 * (g - p)) for p in range(4)]
                moved = jnp.concatenate(pieces, axis=0)
            else:
                tile, at = source(z, i)
                moved = turned(tile, 32 * (g - at))
            value = moved if value is None else jnp.where(lane < 32 * g, value, moved)
        out_ref[:, t * LANES : (t + 1) * LANES] = value


def unpack(returned):
    vmem = pl.BlockSpec(memory_space=pltpu.VMEM)
    return pl.pallas_call(
        unpack_kernel,
        out_shape=jax.ShapeDtypeStruct((OWN, D), jnp.bfloat16),
        in_specs=[vmem],
        out_specs=vmem,
        compiler_params=pltpu.CompilerParams(vmem_limit_bytes=8 * 1024 * 1024),
        name="unpack",
    )(returned)


def body(projected, segment_ids, widths):
    seg_rows = segment_ids.reshape(SEG_ROWS, LANES)
    in_hbm = [pltpu.with_memory_space_constraint(a, pltpu.HBM) for a in (projected, seg_rows, widths.reshape(1, SAMPLES))]
    kv, q = pack(*in_hbm)
    kv = lax.all_to_all(kv, "head", 0, 0, tiled=True)
    kv, q = lax.optimization_barrier((kv, q))
    own = kv.reshape(SHARD, KV_LANES)
    up = [(i, (i + 1) % SEQ) for i in range(SEQ)]
    down = [(j, i) for i, j in up]
    prev = lax.ppermute(own, "seq", up)
    following = lax.ppermute(own, "seq", down)
    q = lax.all_to_all(q, "head", 0, 0, tiled=True)
    out = attend(prev, own, following, q.reshape(SHARD, Q_LANES), seg_rows)
    out = lax.all_to_all(out, "head", 0, 0, tiled=True)
    return unpack(out)


def solution(mesh):
    in_specs = (P(("seq", "head"), None), P(), P())
    out_specs = P(("seq", "head"), None)
    return jax.shard_map(body, mesh=mesh, in_specs=in_specs, out_specs=out_specs, check_vma=False)
```

```python
import math

import jax
import jax.numpy as jnp
import numpy as np
from jax import lax
from jax.experimental import pallas as pl
from jax.experimental.pallas import tpu as pltpu
from jax.sharding import PartitionSpec as P

D = 2304
HEADS = 24
HD = 96
TOKENS = 49152
SAMPLES = 64
GROUP = 8
SEQ = 32
OWN = 192
SHARD = OWN * GROUP
LANES = 128
SEG_ROWS = TOKENS // LANES
SHARD_ROWS = SHARD // LANES

KV_LANES = 5 * LANES
Q_LANES = 2 * LANES
CODE = 64
BITS = 6
ONE = CODE + 2 * BITS
BIG = float(2**20)
BQ = 2 * OWN
BLOCKS = SHARD // BQ
UNIT = 256
MAX_UNITS = 14
STEPS = (7, 6, 5, 4, 3, 2, 1)
CHUNK = 256
PACK_ROWS = 64
SEG_WINDOW = 24
WINDOW = 3 * SHARD
OUT_ROWS = 2 * OWN + OWN // 4
SCALE = math.log2(math.e) / math.sqrt(HD)


def lane_iota(shape, dtype=jnp.int32):
    return lax.broadcasted_iota(dtype, shape, len(shape) - 1)


def turned(x, amount):
    amount %= LANES
    return x if amount == 0 else pltpu.roll(x, amount, 1)


def id_window(seg_ref, ids_ref, sem):
    first_row = jnp.maximum(device_index() * OWN // LANES - SHARD_ROWS, 0)
    base = pl.multiple_of(jnp.minimum(first_row // 8 * 8, SEG_ROWS - SEG_WINDOW), 8)
    return base, pltpu.make_async_copy(seg_ref.at[pl.ds(base, SEG_WINDOW), :], ids_ref, sem)


def device_index():
    return lax.axis_index("seq") * GROUP + lax.axis_index("head")


def row_copies(x_ref, rows_ref, sems):
    count = OWN // PACK_ROWS
    parts = [pl.ds(i * PACK_ROWS, PACK_ROWS) for i in range(count)]
    return [pltpu.make_async_copy(x_ref.at[p, :], rows_ref.at[p, :], sems.at[i]) for i, p in enumerate(parts)]


def swap_matrix():
    source = lax.broadcasted_iota(jnp.int32, (LANES, LANES), 0)
    target = lane_iota((LANES, LANES))
    partner = jnp.where((target % (HD // 2)) < HD // 4, target + HD // 4, target - HD // 4)
    return jnp.where((source == partner) & (target < HD), 1.0, 0.0).astype(jnp.bfloat16)


def row_tools(rows_ref, at, cos, sin, swap):
    lane = lane_iota((PACK_ROWS, LANES))

    def tile(t):
        return rows_ref[at, t * LANES : (t + 1) * LANES]

    def granules(base, count, target):
        t, g = base // LANES, base % LANES
        value = turned(tile(t), target - g)
        if g + 32 * count > LANES:
            cut = target + LANES - g
            value = jnp.where(lane < cut, value, turned(tile(t + 1), target - g))
        return value

    def rope(base):
        x = granules(base, 3, 0)
        other = jnp.dot(x, swap, preferred_element_type=jnp.float32)
        return (x.astype(jnp.float32) * cos + other * sin).astype(jnp.bfloat16)

    return lane, granules, rope


def pack_kernel(
    x_ref, seg_ref, widths_ref, kv_ref, q_ref, cos_ref, sin_ref, code_ref, rows_ref, ids_ref, wide_ref, row_sems, sems
):
    base, ids_copy = id_window(seg_ref, ids_ref, sems.at[0])
    widths_copy = pltpu.make_async_copy(widths_ref, wide_ref, sems.at[1])
    ids_copy.start()
    widths_copy.start()
    copies = row_copies(x_ref, rows_ref, row_sems)
    for copy in copies:
        copy.start()
    first_tok = device_index() * OWN
    rows = lax.broadcasted_iota(jnp.int32, (OWN, 1), 0)
    lanes = lane_iota((1, LANES))
    freq = jnp.zeros((1, LANES), jnp.float32)
    quarter = HD // 4
    for j in range(quarter):
        freq = jnp.where(lanes % quarter == j, float(np.float32(10000.0 ** (-j / quarter))), freq)
    swap = swap_matrix()
    ids_copy.wait()
    widths_copy.wait()
    own = jnp.zeros((OWN, LANES), jnp.float32)
    window = [(ids_ref[r : r + 1, :].astype(jnp.float32), (base + r) * LANES + lanes - first_tok) for r in range(SEG_WINDOW)]
    for ids, place in window:
        own = own + jnp.where(place == rows, ids, 0.0)
    own = jnp.sum(own, axis=1, keepdims=True)
    before = jnp.zeros((OWN, LANES), jnp.float32)
    for ids, place in window:
        before = before + jnp.where((ids == own) & (place < rows), 1.0, 0.0)
    offset = jnp.sum(before, axis=1, keepdims=True)
    samples = lane_iota((1, SAMPLES)).astype(jnp.float32)
    width = jnp.sum(jnp.where(own == samples, wide_ref[...].astype(jnp.float32), 0.0), axis=1, keepdims=True)
    row_pos = jnp.floor((offset + 0.5) / width)
    col_pos = offset - row_pos * width
    angle = jnp.where(lanes < HD // 2, row_pos, col_pos) * freq
    sine = jnp.sin(angle)
    cos_ref[...] = jnp.cos(angle)
    sin_ref[...] = jnp.where((lanes % (HD // 2)) < quarter, -sine, sine)
    ids = own.astype(jnp.int32)
    shift = jnp.clip(jnp.where(lanes < CODE + BITS, lanes - CODE, lanes - CODE - BITS), 0, BITS - 1)
    bit = (ids >> shift) & 1
    code = jnp.where(lanes < CODE + BITS, 1 - bit, bit)
    code = jnp.where(lanes == ONE, 1, jnp.where((lanes >= CODE) & (lanes < ONE), code, 0))
    code_ref[...] = code.astype(jnp.float32).astype(jnp.bfloat16)
    for copy in copies:
        copy.wait()

    def step(i, carry):
        at = pl.ds(pl.multiple_of(i * PACK_ROWS, PACK_ROWS), PACK_ROWS)
        lane, granules, rope = row_tools(rows_ref, at, cos_ref[at, :], sin_ref[at, :], swap)
        for z in range(GROUP):
            q0 = z * 3 * HD
            k0, v0 = D + q0, 2 * D + q0
            for h in range(3):
                kv_ref[z, at, h * LANES : (h + 1) * LANES] = jnp.where(
                    lane < HD, rope(k0 + h * HD), granules(v0 + 32 * h, 1, HD)
                )
            kv_ref[z, at, 3 * LANES : 4 * LANES] = jnp.where(
                lane < HD, granules(v0 + HD, 3, 0), granules(v0 + 2 * HD, 1, HD)
            )
            q2 = rope(q0 + 2 * HD)
            tail = jnp.where(lane < HD, code_ref[at, :], turned(q2, 32))
            kv_ref[z, at, 4 * LANES : 5 * LANES] = jnp.where(lane < CODE, granules(v0 + 2 * HD + 32, 2, 0), tail)
            q_ref[z, at, :LANES] = jnp.where(lane < HD, rope(q0), turned(q2, HD))
            q_ref[z, at, LANES:] = jnp.where(lane < HD, rope(q0 + HD), turned(q2, 64))
        return carry

    lax.fori_loop(0, OWN // PACK_ROWS, step, 0)


def pack(projected, seg_rows, widths_row):
    vmem, hbm = pl.BlockSpec(memory_space=pltpu.VMEM), pl.BlockSpec(memory_space=pltpu.HBM)
    return pl.pallas_call(
        pack_kernel,
        out_shape=[
            jax.ShapeDtypeStruct((GROUP, OWN, KV_LANES), jnp.bfloat16),
            jax.ShapeDtypeStruct((GROUP, OWN, Q_LANES), jnp.bfloat16),
        ],
        in_specs=[hbm] * 3,
        out_specs=[vmem] * 2,
        scratch_shapes=[
            pltpu.VMEM((OWN, LANES), jnp.float32),
            pltpu.VMEM((OWN, LANES), jnp.float32),
            pltpu.VMEM((OWN, LANES), jnp.bfloat16),
            pltpu.VMEM((OWN, 3 * D), jnp.bfloat16),
            pltpu.VMEM((SEG_WINDOW, LANES), jnp.int32),
            pltpu.VMEM((1, SAMPLES), jnp.int32),
            pltpu.SemaphoreType.DMA((OWN // PACK_ROWS,)),
            pltpu.SemaphoreType.DMA((2,)),
        ],
        compiler_params=pltpu.CompilerParams(vmem_limit_bytes=10 * 1024 * 1024),
        name="pack",
    )(projected, seg_rows, widths_row)


def key_ranges(seg_ref, start_ref, count_ref):
    shard = lax.axis_index("seq")

    def ids_of(index):
        return seg_ref[pl.ds(pl.multiple_of(index * SHARD_ROWS, 4), SHARD_ROWS), :].astype(jnp.float32)

    own_ids = ids_of(shard)
    prev_ids = jnp.where(shard > 0, ids_of(jnp.maximum(shard - 1, 0)), -1.0)
    next_ids = jnp.where(shard < SEQ - 1, ids_of(jnp.minimum(shard + 1, SEQ - 1)), -1.0)
    place = lax.broadcasted_iota(jnp.int32, (SHARD_ROWS, LANES), 0) * LANES + lane_iota((SHARD_ROWS, LANES))

    def total(x):
        return jnp.sum(jnp.sum(x, axis=0, keepdims=True), axis=1, keepdims=True)

    begin, end = WINDOW, 0
    for b in range(BLOCKS):
        first = total(jnp.where(place == b * BQ, own_ids, 0.0))
        last = total(jnp.where(place == b * BQ + BQ - 1, own_ids, 0.0))
        low = total(jnp.where(own_ids < first, 1.0, 0.0) - jnp.where(prev_ids == first, 1.0, 0.0))
        high = total(jnp.where(own_ids <= last, 1.0, 0.0) + jnp.where(next_ids == last, 1.0, 0.0))
        lo, hi = low[0, 0].astype(jnp.int32) + SHARD, high[0, 0].astype(jnp.int32) + SHARD
        start = lo // LANES * LANES
        count = (hi - start + UNIT - 1) // UNIT
        start = jnp.minimum(start, WINDOW - count * UNIT)
        start_ref[b] = start
        count_ref[b] = count
        begin = jnp.minimum(begin, start)
        end = jnp.maximum(end, start + count * UNIT)
    return begin, end


def gather_keys(prev_ref, own_ref, next_ref, seg_ref, kv_ref, v0_ref, start_ref, count_ref):
    begin, end = key_ranges(seg_ref, start_ref, count_ref)
    first_chunk, last_chunk = begin // CHUNK, (end + CHUNK - 1) // CHUNK
    shard_chunks = SHARD // CHUNK

    def copy_from(ref, number):
        low, high = number * shard_chunks, (number + 1) * shard_chunks

        def move(i, carry):
            src = pl.ds(pl.multiple_of((i - low) * CHUNK, CHUNK), CHUNK)
            dst = pl.ds(pl.multiple_of(i * CHUNK, CHUNK), CHUNK)
            lane = lane_iota((CHUNK, LANES))
            parts = []
            for t in range(5):
                value = ref[src, t * LANES : (t + 1) * LANES]
                kv_ref[dst, t * LANES : (t + 1) * LANES] = value
                parts.append(value)
            v0 = jnp.where(lane < 32, turned(parts[0], 32), jnp.where(lane < 64, turned(parts[1], 64), turned(parts[2], 96)))
            v0_ref[dst, :] = jnp.where(lane < HD, v0, jnp.where(lane == HD, 1.0, 0.0).astype(jnp.bfloat16))
            return carry

        lax.fori_loop(jnp.clip(first_chunk, low, high), jnp.clip(last_chunk, low, high), move, 0)

    copy_from(prev_ref, 0)
    copy_from(own_ref, 1)
    copy_from(next_ref, 2)


def attend_kernel(
    prev_ref, own_ref, next_ref, q_ref, seg_ref, out_ref, kv_ref, v0_ref, qa_ref, qc_ref, start_ref, count_ref, *work
):
    gather_keys(prev_ref, own_ref, next_ref, seg_ref, kv_ref, v0_ref, start_ref, count_ref)
    m_refs, o_refs, s_refs = work[:3], work[3:6], work[6:]
    o0_ref, o1_ref, o2_ref = o_refs

    def arrange(b, carry):
        at = pl.ds(pl.multiple_of(b * BQ, BQ), BQ)
        lane = lane_iota((BQ, LANES))
        zero = jnp.zeros((BQ, LANES), jnp.bfloat16)
        t4 = own_ref[at, 4 * LANES :]
        t5 = q_ref[at, :LANES]
        t6 = q_ref[at, LANES:]
        qa_ref[0, at, :] = jnp.where(lane < HD, t5, zero)
        qa_ref[1, at, :] = jnp.where(lane < HD, t6, zero)
        q2 = jnp.where(lane < 32, turned(t5, 32), jnp.where(lane < 64, turned(t6, 64), turned(t4, 96)))
        qa_ref[2, at, :] = jnp.where(lane < HD, q2, zero)
        other = (t4.astype(jnp.float32) - 1.0) * BIG
        qc_ref[at, :] = jnp.where((lane >= CODE) & (lane < ONE), other, 0.0).astype(jnp.bfloat16)
        return carry

    lax.fori_loop(0, BLOCKS, arrange, 0)

    def block(b, carry):
        start, count = start_ref[b], count_ref[b]
        at = pl.ds(pl.multiple_of(b * BQ, BQ), BQ)

        def scores(first_unit, size, j, heads=(0, 1, 2), fresh=False):
            keys = pl.ds(pl.multiple_of(start + first_unit * UNIT + j * size, LANES), size)
            t4 = kv_ref[keys, 4 * LANES :]
            for h in heads:
                k = jnp.concatenate([kv_ref[keys, h * LANES : (h + 1) * LANES], t4], axis=1)
                q = jnp.concatenate([qa_ref[h, at, :], qc_ref[at, :]], axis=1)
                s = lax.dot_general(q, k, (((1,), (1,)), ((), ())), preferred_element_type=jnp.float32)
                for u in range(size // UNIT):
                    s_refs[h][first_unit + j * (size // UNIT) + u] = s[:, u * UNIT : (u + 1) * UNIT]
                top = s[:, :LANES]
                for t in range(1, size // LANES):
                    top = jnp.maximum(top, s[:, t * LANES : (t + 1) * LANES])
                m_refs[h][...] = top if fresh else jnp.maximum(m_refs[h][...], top)

        def blend(first_unit, size, j, heads=(0, 1, 2), fresh=False):
            keys = pl.ds(pl.multiple_of(start + first_unit * UNIT + j * size, LANES), size)
            for h in heads:
                m = jnp.concatenate([m_refs[h][...]] * (UNIT // LANES), axis=1)
                weights = jnp.concatenate(
                    [
                        jnp.exp2(s_refs[h][first_unit + j * (size // UNIT) + u] * SCALE - m).astype(jnp.bfloat16)
                        for u in range(size // UNIT)
                    ],
                    axis=1,
                )
                values = v0_ref[keys, :] if h == 0 else kv_ref[keys, 3 * LANES :]
                blended = jnp.dot(weights, values, preferred_element_type=jnp.float32)
                o_refs[h][...] = blended if fresh else o_refs[h][...] + blended

        def over_keys(what):
            done = 0
            for units in STEPS:
                steps = (count - done) // units
                lax.fori_loop(0, steps, lambda j, c: what(done, units * UNIT, j) or c, 0)
                done = done + steps * units

        def settle(h):
            m_refs[h][...] = jnp.broadcast_to(jnp.max(m_refs[h][...], axis=1, keepdims=True) * SCALE, (BQ, LANES))

        for units in STEPS:

            @pl.when(count == units)
            def _(size=units * UNIT):
                scores(0, size, 0, fresh=True)
                for h in range(3):
                    settle(h)
                blend(0, size, 0, fresh=True)

        @pl.when(count > max(STEPS))
        def _():
            for ref in m_refs:
                ref[...] = jnp.full_like(ref, -3.0e38)
            for ref in o_refs:
                ref[...] = jnp.zeros_like(ref)
            over_keys(scores)
            for h in range(3):
                settle(h)
            over_keys(blend)

        lane = lane_iota((OWN, LANES))
        part = OWN // 4
        part_lane = lane_iota((part, LANES))
        for i in range(BQ // OWN):
            at = slice(i * OWN, (i + 1) * OWN)
            to = b * (BQ // OWN) + i
            o0 = o0_ref[at, :]
            o0 = o0 * (1.0 / o0[:, HD : HD + 1])
            o1 = o1_ref[at, :LANES] * (1.0 / o1_ref[at, LANES:][:, ONE : ONE + 1])
            o2a, o2b = o2_ref[at, :LANES], o2_ref[at, LANES:]
            r2 = 1.0 / o2b[:, ONE : ONE + 1]
            o2a, o2b = o2a * r2, o2b * r2
            out_ref[to, :OWN, :] = jnp.where(lane < HD, o0, o2a).astype(jnp.bfloat16)
            out_ref[to, OWN : 2 * OWN, :] = jnp.where(lane < HD, o1, turned(o2b, 96)).astype(jnp.bfloat16)
            fold = turned(o2b[:part], 96)
            for g in range(1, 4):
                fold = jnp.where(part_lane < 32 * g, fold, turned(o2b[g * part : (g + 1) * part], 32 * g - 32))
            out_ref[to, 2 * OWN :, :] = fold.astype(jnp.bfloat16)
        return carry

    lax.fori_loop(0, BLOCKS, block, 0)


def attend(prev, own, following, queries, seg_rows):
    vmem = pl.BlockSpec(memory_space=pltpu.VMEM)
    return pl.pallas_call(
        attend_kernel,
        out_shape=jax.ShapeDtypeStruct((GROUP, OUT_ROWS, LANES), jnp.bfloat16),
        in_specs=[vmem] * 5,
        out_specs=vmem,
        scratch_shapes=[
            pltpu.VMEM((WINDOW, KV_LANES), jnp.bfloat16),
            pltpu.VMEM((WINDOW, LANES), jnp.bfloat16),
            pltpu.VMEM((3, SHARD, LANES), jnp.bfloat16),
            pltpu.VMEM((SHARD, LANES), jnp.bfloat16),
            pltpu.SMEM((BLOCKS,), jnp.int32),
            pltpu.SMEM((BLOCKS,), jnp.int32),
            *[pltpu.VMEM((BQ, LANES), jnp.float32)] * 4,
            *[pltpu.VMEM((BQ, 2 * LANES), jnp.float32)] * 2,
            *[pltpu.VMEM((MAX_UNITS, BQ, UNIT), jnp.float32)] * 3,
        ],
        compiler_params=pltpu.CompilerParams(vmem_limit_bytes=40 * 1024 * 1024),
        name="attend",
    )(prev, own, following, queries, seg_rows)


def unpack_kernel(in_ref, out_ref):
    lane = lane_iota((OWN, LANES))
    part = OWN // 4

    def source(z, i):
        if i < 3:
            return in_ref[z, :OWN, :], i
        if i < 6:
            return in_ref[z, OWN : 2 * OWN, :], i - 3
        return in_ref[z, (i - 6) * OWN : (i - 5) * OWN, :], 3

    for t in range(D // LANES):
        value = None
        for g in range(4):
            z, i = divmod(4 * t + g, 9)
            if i == 8:
                pieces = [turned(in_ref[z, 2 * OWN :, :], 32 * (g - p)) for p in range(4)]
                moved = jnp.concatenate(pieces, axis=0)
            else:
                tile, at = source(z, i)
                moved = turned(tile, 32 * (g - at))
            value = moved if value is None else jnp.where(lane < 32 * g, value, moved)
        out_ref[:, t * LANES : (t + 1) * LANES] = value


def unpack(returned):
    vmem = pl.BlockSpec(memory_space=pltpu.VMEM)
    return pl.pallas_call(
        unpack_kernel,
        out_shape=jax.ShapeDtypeStruct((OWN, D), jnp.bfloat16),
        in_specs=[vmem],
        out_specs=vmem,
        compiler_params=pltpu.CompilerParams(vmem_limit_bytes=8 * 1024 * 1024),
        name="unpack",
    )(returned)


def body(projected, segment_ids, widths):
    seg_rows = segment_ids.reshape(SEG_ROWS, LANES)
    in_hbm = [pltpu.with_memory_space_constraint(a, pltpu.HBM) for a in (projected, seg_rows, widths.reshape(1, SAMPLES))]
    kv, q = pack(*in_hbm)
    kv = lax.all_to_all(kv, "head", 0, 0, tiled=True)
    kv, q = lax.optimization_barrier((kv, q))
    own = kv.reshape(SHARD, KV_LANES)
    up = [(i, (i + 1) % SEQ) for i in range(SEQ)]
    down = [(j, i) for i, j in up]
    prev = lax.ppermute(own, "seq", up)
    following = lax.ppermute(own, "seq", down)
    q = lax.all_to_all(q, "head", 0, 0, tiled=True)
    out = attend(prev, own, following, q.reshape(SHARD, Q_LANES), seg_rows)
    out = lax.all_to_all(out, "head", 0, 0, tiled=True)
    return unpack(out)


def solution(mesh):
    in_specs = (P(("seq", "head"), None), P(), P())
    out_specs = P(("seq", "head"), None)
    return jax.shard_map(body, mesh=mesh, in_specs=in_specs, out_specs=out_specs, check_vma=False)
```

```python
import math

import jax
import jax.numpy as jnp
import numpy as np
from jax import lax
from jax.experimental import pallas as pl
from jax.experimental.pallas import tpu as pltpu
from jax.sharding import PartitionSpec as P

D = 2304
HEADS = 24
HD = 96
TOKENS = 49152
SAMPLES = 64
GROUP = 8
SEQ = 32
OWN = 192
SHARD = OWN * GROUP
LANES = 128
SEG_ROWS = TOKENS // LANES
SHARD_ROWS = SHARD // LANES

KV_LANES = 5 * LANES
Q_LANES = 2 * LANES
CODE = 64
BITS = 6
ONE = CODE + 2 * BITS
BIG = float(2**20)
BQ = 2 * OWN
BLOCKS = SHARD // BQ
UNIT = 256
MAX_UNITS = 14
STEPS = (7, 6, 5, 4, 3, 2, 1)
CHUNK = 512
PACK_ROWS = 64
SEG_WINDOW = 24
WINDOW = 3 * SHARD
OUT_ROWS = 2 * OWN + OWN // 4
SCALE = math.log2(math.e) / math.sqrt(HD)


def lane_iota(shape, dtype=jnp.int32):
    return lax.broadcasted_iota(dtype, shape, len(shape) - 1)


def turned(x, amount):
    amount %= LANES
    return x if amount == 0 else pltpu.roll(x, amount, 1)


def id_window(seg_ref, ids_ref, sem):
    first_row = jnp.maximum(device_index() * OWN // LANES - SHARD_ROWS, 0)
    base = pl.multiple_of(jnp.minimum(first_row // 8 * 8, SEG_ROWS - SEG_WINDOW), 8)
    return base, pltpu.make_async_copy(seg_ref.at[pl.ds(base, SEG_WINDOW), :], ids_ref, sem)


def device_index():
    return lax.axis_index("seq") * GROUP + lax.axis_index("head")


def row_copies(x_ref, rows_ref, sems):
    count = OWN // PACK_ROWS
    parts = [pl.ds(i * PACK_ROWS, PACK_ROWS) for i in range(count)]
    return [pltpu.make_async_copy(x_ref.at[p, :], rows_ref.at[p, :], sems.at[i]) for i, p in enumerate(parts)]


def swap_matrix():
    source = lax.broadcasted_iota(jnp.int32, (LANES, LANES), 0)
    target = lane_iota((LANES, LANES))
    partner = jnp.where((target % (HD // 2)) < HD // 4, target + HD // 4, target - HD // 4)
    return jnp.where((source == partner) & (target < HD), 1.0, 0.0).astype(jnp.bfloat16)


def row_tools(rows_ref, at, cos, sin, swap):
    lane = lane_iota((PACK_ROWS, LANES))

    def tile(t):
        return rows_ref[at, t * LANES : (t + 1) * LANES]

    def granules(base, count, target):
        t, g = base // LANES, base % LANES
        value = turned(tile(t), target - g)
        if g + 32 * count > LANES:
            cut = target + LANES - g
            value = jnp.where(lane < cut, value, turned(tile(t + 1), target - g))
        return value

    def rope(base):
        x = granules(base, 3, 0)
        other = jnp.dot(x, swap, preferred_element_type=jnp.float32)
        return (x.astype(jnp.float32) * cos + other * sin).astype(jnp.bfloat16)

    return lane, granules, rope


def pack_kernel(
    x_ref, seg_ref, widths_ref, kv_ref, q_ref, cos_ref, sin_ref, code_ref, rows_ref, ids_ref, wide_ref, row_sems, sems
):
    base, ids_copy = id_window(seg_ref, ids_ref, sems.at[0])
    widths_copy = pltpu.make_async_copy(widths_ref, wide_ref, sems.at[1])
    ids_copy.start()
    widths_copy.start()
    copies = row_copies(x_ref, rows_ref, row_sems)
    for copy in copies:
        copy.start()
    first_tok = device_index() * OWN
    rows = lax.broadcasted_iota(jnp.int32, (OWN, 1), 0)
    lanes = lane_iota((1, LANES))
    freq = jnp.zeros((1, LANES), jnp.float32)
    quarter = HD // 4
    for j in range(quarter):
        freq = jnp.where(lanes % quarter == j, float(np.float32(10000.0 ** (-j / quarter))), freq)
    swap = swap_matrix()
    ids_copy.wait()
    widths_copy.wait()
    own = jnp.zeros((OWN, LANES), jnp.float32)
    window = [(ids_ref[r : r + 1, :].astype(jnp.float32), (base + r) * LANES + lanes - first_tok) for r in range(SEG_WINDOW)]
    for ids, place in window:
        own = own + jnp.where(place == rows, ids, 0.0)
    own = jnp.sum(own, axis=1, keepdims=True)
    before = jnp.zeros((OWN, LANES), jnp.float32)
    for ids, place in window:
        before = before + jnp.where((ids == own) & (place < rows), 1.0, 0.0)
    offset = jnp.sum(before, axis=1, keepdims=True)
    samples = lane_iota((1, SAMPLES)).astype(jnp.float32)
    width = jnp.sum(jnp.where(own == samples, wide_ref[...].astype(jnp.float32), 0.0), axis=1, keepdims=True)
    row_pos = jnp.floor((offset + 0.5) / width)
    col_pos = offset - row_pos * width
    angle = jnp.where(lanes < HD // 2, row_pos, col_pos) * freq
    sine = jnp.sin(angle)
    cos_ref[...] = jnp.cos(angle)
    sin_ref[...] = jnp.where((lanes % (HD // 2)) < quarter, -sine, sine)
    ids = own.astype(jnp.int32)
    shift = jnp.clip(jnp.where(lanes < CODE + BITS, lanes - CODE, lanes - CODE - BITS), 0, BITS - 1)
    bit = (ids >> shift) & 1
    code = jnp.where(lanes < CODE + BITS, 1 - bit, bit)
    code = jnp.where(lanes == ONE, 1, jnp.where((lanes >= CODE) & (lanes < ONE), code, 0))
    code_ref[...] = code.astype(jnp.float32).astype(jnp.bfloat16)
    for copy in copies:
        copy.wait()

    def step(i, carry):
        at = pl.ds(pl.multiple_of(i * PACK_ROWS, PACK_ROWS), PACK_ROWS)
        lane, granules, rope = row_tools(rows_ref, at, cos_ref[at, :], sin_ref[at, :], swap)
        for z in range(GROUP):
            q0 = z * 3 * HD
            k0, v0 = D + q0, 2 * D + q0
            for h in range(3):
                kv_ref[z, at, h * LANES : (h + 1) * LANES] = jnp.where(
                    lane < HD, rope(k0 + h * HD), granules(v0 + 32 * h, 1, HD)
                )
            kv_ref[z, at, 3 * LANES : 4 * LANES] = jnp.where(
                lane < HD, granules(v0 + HD, 3, 0), granules(v0 + 2 * HD, 1, HD)
            )
            q2 = rope(q0 + 2 * HD)
            tail = jnp.where(lane < HD, code_ref[at, :], turned(q2, 32))
            kv_ref[z, at, 4 * LANES : 5 * LANES] = jnp.where(lane < CODE, granules(v0 + 2 * HD + 32, 2, 0), tail)
            q_ref[z, at, :LANES] = jnp.where(lane < HD, rope(q0), turned(q2, HD))
            q_ref[z, at, LANES:] = jnp.where(lane < HD, rope(q0 + HD), turned(q2, 64))
        return carry

    lax.fori_loop(0, OWN // PACK_ROWS, step, 0)


def pack(projected, seg_rows, widths_row):
    vmem, hbm = pl.BlockSpec(memory_space=pltpu.VMEM), pl.BlockSpec(memory_space=pltpu.HBM)
    return pl.pallas_call(
        pack_kernel,
        out_shape=[
            jax.ShapeDtypeStruct((GROUP, OWN, KV_LANES), jnp.bfloat16),
            jax.ShapeDtypeStruct((GROUP, OWN, Q_LANES), jnp.bfloat16),
        ],
        in_specs=[hbm] * 3,
        out_specs=[vmem] * 2,
        scratch_shapes=[
            pltpu.VMEM((OWN, LANES), jnp.float32),
            pltpu.VMEM((OWN, LANES), jnp.float32),
            pltpu.VMEM((OWN, LANES), jnp.bfloat16),
            pltpu.VMEM((OWN, 3 * D), jnp.bfloat16),
            pltpu.VMEM((SEG_WINDOW, LANES), jnp.int32),
            pltpu.VMEM((1, SAMPLES), jnp.int32),
            pltpu.SemaphoreType.DMA((OWN // PACK_ROWS,)),
            pltpu.SemaphoreType.DMA((2,)),
        ],
        compiler_params=pltpu.CompilerParams(vmem_limit_bytes=10 * 1024 * 1024),
        name="pack",
    )(projected, seg_rows, widths_row)


def key_ranges(seg_ref, start_ref, count_ref):
    shard = lax.axis_index("seq")

    def ids_of(index):
        return seg_ref[pl.ds(pl.multiple_of(index * SHARD_ROWS, 4), SHARD_ROWS), :].astype(jnp.float32)

    own_ids = ids_of(shard)
    prev_ids = jnp.where(shard > 0, ids_of(jnp.maximum(shard - 1, 0)), -1.0)
    next_ids = jnp.where(shard < SEQ - 1, ids_of(jnp.minimum(shard + 1, SEQ - 1)), -1.0)
    place = lax.broadcasted_iota(jnp.int32, (SHARD_ROWS, LANES), 0) * LANES + lane_iota((SHARD_ROWS, LANES))

    def total(x):
        return jnp.sum(jnp.sum(x, axis=0, keepdims=True), axis=1, keepdims=True)

    begin, end = WINDOW, 0
    for b in range(BLOCKS):
        first = total(jnp.where(place == b * BQ, own_ids, 0.0))
        last = total(jnp.where(place == b * BQ + BQ - 1, own_ids, 0.0))
        low = total(jnp.where(own_ids < first, 1.0, 0.0) - jnp.where(prev_ids == first, 1.0, 0.0))
        high = total(jnp.where(own_ids <= last, 1.0, 0.0) + jnp.where(next_ids == last, 1.0, 0.0))
        lo, hi = low[0, 0].astype(jnp.int32) + SHARD, high[0, 0].astype(jnp.int32) + SHARD
        start = lo // LANES * LANES
        count = (hi - start + UNIT - 1) // UNIT
        start = jnp.minimum(start, WINDOW - count * UNIT)
        start_ref[b] = start
        count_ref[b] = count
        begin = jnp.minimum(begin, start)
        end = jnp.maximum(end, start + count * UNIT)
    return begin, end


def gather_keys(prev_ref, own_ref, next_ref, seg_ref, kv_ref, v0_ref, start_ref, count_ref):
    begin, end = key_ranges(seg_ref, start_ref, count_ref)
    first_chunk, last_chunk = begin // CHUNK, (end + CHUNK - 1) // CHUNK
    shard_chunks = SHARD // CHUNK

    def copy_from(ref, number):
        low, high = number * shard_chunks, (number + 1) * shard_chunks

        def move(i, carry):
            src = pl.ds(pl.multiple_of((i - low) * CHUNK, CHUNK), CHUNK)
            dst = pl.ds(pl.multiple_of(i * CHUNK, CHUNK), CHUNK)
            lane = lane_iota((CHUNK, LANES))
            parts = []
            for t in range(5):
                value = ref[src, t * LANES : (t + 1) * LANES]
                kv_ref[dst, t * LANES : (t + 1) * LANES] = value
                parts.append(value)
            v0 = jnp.where(lane < 32, turned(parts[0], 32), jnp.where(lane < 64, turned(parts[1], 64), turned(parts[2], 96)))
            v0_ref[dst, :] = jnp.where(lane < HD, v0, jnp.where(lane == HD, 1.0, 0.0).astype(jnp.bfloat16))
            return carry

        lax.fori_loop(jnp.clip(first_chunk, low, high), jnp.clip(last_chunk, low, high), move, 0)

    copy_from(prev_ref, 0)
    copy_from(own_ref, 1)
    copy_from(next_ref, 2)


def attend_kernel(
    prev_ref, own_ref, next_ref, q_ref, seg_ref, out_ref, kv_ref, v0_ref, qa_ref, qc_ref, start_ref, count_ref, *work
):
    gather_keys(prev_ref, own_ref, next_ref, seg_ref, kv_ref, v0_ref, start_ref, count_ref)
    m_refs, o_refs, s_refs = work[:3], work[3:6], work[6:]
    o0_ref, o1_ref, o2_ref = o_refs

    def arrange(b, carry):
        at = pl.ds(pl.multiple_of(b * BQ, BQ), BQ)
        lane = lane_iota((BQ, LANES))
        zero = jnp.zeros((BQ, LANES), jnp.bfloat16)
        t4 = own_ref[at, 4 * LANES :]
        t5 = q_ref[at, :LANES]
        t6 = q_ref[at, LANES:]
        qa_ref[0, at, :] = jnp.where(lane < HD, t5, zero)
        qa_ref[1, at, :] = jnp.where(lane < HD, t6, zero)
        q2 = jnp.where(lane < 32, turned(t5, 32), jnp.where(lane < 64, turned(t6, 64), turned(t4, 96)))
        qa_ref[2, at, :] = jnp.where(lane < HD, q2, zero)
        other = (t4.astype(jnp.float32) - 1.0) * BIG
        qc_ref[at, :] = jnp.where((lane >= CODE) & (lane < ONE), other, 0.0).astype(jnp.bfloat16)
        return carry

    lax.fori_loop(0, BLOCKS, arrange, 0)

    def block(b, carry):
        start, count = start_ref[b], count_ref[b]
        at = pl.ds(pl.multiple_of(b * BQ, BQ), BQ)

        def scores(first_unit, size, j, heads=(0, 1, 2), fresh=False):
            keys = pl.ds(pl.multiple_of(start + first_unit * UNIT + j * size, LANES), size)
            t4 = kv_ref[keys, 4 * LANES :]
            for h in heads:
                k = jnp.concatenate([kv_ref[keys, h * LANES : (h + 1) * LANES], t4], axis=1)
                q = jnp.concatenate([qa_ref[h, at, :], qc_ref[at, :]], axis=1)
                s = lax.dot_general(q, k, (((1,), (1,)), ((), ())), preferred_element_type=jnp.float32)
                for u in range(size // UNIT):
                    s_refs[h][first_unit + j * (size // UNIT) + u] = s[:, u * UNIT : (u + 1) * UNIT]
                top = s[:, :LANES]
                for t in range(1, size // LANES):
                    top = jnp.maximum(top, s[:, t * LANES : (t + 1) * LANES])
                m_refs[h][...] = top if fresh else jnp.maximum(m_refs[h][...], top)

        def blend(first_unit, size, j, heads=(0, 1, 2), fresh=False):
            keys = pl.ds(pl.multiple_of(start + first_unit * UNIT + j * size, LANES), size)
            for h in heads:
                m = jnp.concatenate([m_refs[h][...]] * (UNIT // LANES), axis=1)
                weights = jnp.concatenate(
                    [
                        jnp.exp2(s_refs[h][first_unit + j * (size // UNIT) + u] * SCALE - m).astype(jnp.bfloat16)
                        for u in range(size // UNIT)
                    ],
                    axis=1,
                )
                values = v0_ref[keys, :] if h == 0 else kv_ref[keys, 3 * LANES :]
                blended = jnp.dot(weights, values, preferred_element_type=jnp.float32)
                o_refs[h][...] = blended if fresh else o_refs[h][...] + blended

        def over_keys(what):
            done = 0
            for units in STEPS:
                steps = (count - done) // units
                lax.fori_loop(0, steps, lambda j, c: what(done, units * UNIT, j) or c, 0)
                done = done + steps * units

        def settle(h):
            m_refs[h][...] = jnp.broadcast_to(jnp.max(m_refs[h][...], axis=1, keepdims=True) * SCALE, (BQ, LANES))

        for units in STEPS:

            @pl.when(count == units)
            def _(size=units * UNIT):
                scores(0, size, 0, fresh=True)
                for h in range(3):
                    settle(h)
                blend(0, size, 0, fresh=True)

        @pl.when(count > max(STEPS))
        def _():
            for ref in m_refs:
                ref[...] = jnp.full_like(ref, -3.0e38)
            for ref in o_refs:
                ref[...] = jnp.zeros_like(ref)
            over_keys(scores)
            for h in range(3):
                settle(h)
            over_keys(blend)

        lane = lane_iota((OWN, LANES))
        part = OWN // 4
        part_lane = lane_iota((part, LANES))
        for i in range(BQ // OWN):
            at = slice(i * OWN, (i + 1) * OWN)
            to = b * (BQ // OWN) + i
            o0 = o0_ref[at, :]
            o0 = o0 * (1.0 / o0[:, HD : HD + 1])
            o1 = o1_ref[at, :LANES] * (1.0 / o1_ref[at, LANES:][:, ONE : ONE + 1])
            o2a, o2b = o2_ref[at, :LANES], o2_ref[at, LANES:]
            r2 = 1.0 / o2b[:, ONE : ONE + 1]
            o2a, o2b = o2a * r2, o2b * r2
            out_ref[to, :OWN, :] = jnp.where(lane < HD, o0, o2a).astype(jnp.bfloat16)
            out_ref[to, OWN : 2 * OWN, :] = jnp.where(lane < HD, o1, turned(o2b, 96)).astype(jnp.bfloat16)
            fold = turned(o2b[:part], 96)
            for g in range(1, 4):
                fold = jnp.where(part_lane < 32 * g, fold, turned(o2b[g * part : (g + 1) * part], 32 * g - 32))
            out_ref[to, 2 * OWN :, :] = fold.astype(jnp.bfloat16)
        return carry

    lax.fori_loop(0, BLOCKS, block, 0)


def attend(prev, own, following, queries, seg_rows):
    vmem = pl.BlockSpec(memory_space=pltpu.VMEM)
    return pl.pallas_call(
        attend_kernel,
        out_shape=jax.ShapeDtypeStruct((GROUP, OUT_ROWS, LANES), jnp.bfloat16),
        in_specs=[vmem] * 5,
        out_specs=vmem,
        scratch_shapes=[
            pltpu.VMEM((WINDOW, KV_LANES), jnp.bfloat16),
            pltpu.VMEM((WINDOW, LANES), jnp.bfloat16),
            pltpu.VMEM((3, SHARD, LANES), jnp.bfloat16),
            pltpu.VMEM((SHARD, LANES), jnp.bfloat16),
            pltpu.SMEM((BLOCKS,), jnp.int32),
            pltpu.SMEM((BLOCKS,), jnp.int32),
            *[pltpu.VMEM((BQ, LANES), jnp.float32)] * 4,
            *[pltpu.VMEM((BQ, 2 * LANES), jnp.float32)] * 2,
            *[pltpu.VMEM((MAX_UNITS, BQ, UNIT), jnp.float32)] * 3,
        ],
        compiler_params=pltpu.CompilerParams(vmem_limit_bytes=40 * 1024 * 1024),
        name="attend",
    )(prev, own, following, queries, seg_rows)


def unpack_kernel(in_ref, out_hbm, out_ref, sems):
    group = 3 * LANES
    copies = []
    lane = lane_iota((OWN, LANES))
    part = OWN // 4

    def source(z, i):
        if i < 3:
            return in_ref[z, :OWN, :], i
        if i < 6:
            return in_ref[z, OWN : 2 * OWN, :], i - 3
        return in_ref[z, (i - 6) * OWN : (i - 5) * OWN, :], 3

    for t in range(D // LANES):
        value = None
        for g in range(4):
            z, i = divmod(4 * t + g, 9)
            if i == 8:
                pieces = [turned(in_ref[z, 2 * OWN :, :], 32 * (g - p)) for p in range(4)]
                moved = jnp.concatenate(pieces, axis=0)
            else:
                tile, at = source(z, i)
                moved = turned(tile, 32 * (g - at))
            value = moved if value is None else jnp.where(lane < 32 * g, value, moved)
        out_ref[:, t * LANES : (t + 1) * LANES] = value
        if (t + 1) * LANES % group == 0:
            done = pl.ds((t + 1) * LANES - group, group)
            copies.append(pltpu.make_async_copy(out_ref.at[:, done], out_hbm.at[:, done], sems.at[len(copies)]))
            copies[-1].start()
    for copy in copies:
        copy.wait()


def unpack(returned):
    vmem = pl.BlockSpec(memory_space=pltpu.VMEM)
    return pl.pallas_call(
        unpack_kernel,
        out_shape=jax.ShapeDtypeStruct((OWN, D), jnp.bfloat16),
        in_specs=[vmem],
        out_specs=pl.BlockSpec(memory_space=pltpu.HBM),
        scratch_shapes=[pltpu.VMEM((OWN, D), jnp.bfloat16), pltpu.SemaphoreType.DMA((D // (3 * LANES),))],
        compiler_params=pltpu.CompilerParams(vmem_limit_bytes=8 * 1024 * 1024),
        name="unpack",
    )(returned)


def body(projected, segment_ids, widths):
    seg_rows = segment_ids.reshape(SEG_ROWS, LANES)
    in_hbm = [pltpu.with_memory_space_constraint(a, pltpu.HBM) for a in (projected, seg_rows, widths.reshape(1, SAMPLES))]
    kv, q = pack(*in_hbm)
    kv = lax.all_to_all(kv, "head", 0, 0, tiled=True)
    kv, q = lax.optimization_barrier((kv, q))
    own = kv.reshape(SHARD, KV_LANES)
    up = [(i, (i + 1) % SEQ) for i in range(SEQ)]
    down = [(j, i) for i, j in up]
    prev = lax.ppermute(own, "seq", up)
    following = lax.ppermute(own, "seq", down)
    q = lax.all_to_all(q, "head", 0, 0, tiled=True)
    out = attend(prev, own, following, q.reshape(SHARD, Q_LANES), seg_rows)
    out = lax.all_to_all(out, "head", 0, 0, tiled=True)
    return unpack(out)


def solution(mesh):
    in_specs = (P(("seq", "head"), None), P(), P())
    out_specs = P(("seq", "head"), None)
    return jax.shard_map(body, mesh=mesh, in_specs=in_specs, out_specs=out_specs, check_vma=False)
```

```python
import math

import jax
import jax.numpy as jnp
import numpy as np
from jax import lax
from jax.experimental import pallas as pl
from jax.experimental.pallas import tpu as pltpu
from jax.sharding import PartitionSpec as P

D = 2304
HEADS = 24
HD = 96
TOKENS = 49152
SAMPLES = 64
GROUP = 8
SEQ = 32
OWN = 192
SHARD = OWN * GROUP
LANES = 128
SEG_ROWS = TOKENS // LANES
SHARD_ROWS = SHARD // LANES

KV_LANES = 5 * LANES
Q_LANES = 2 * LANES
CODE = 64
BITS = 6
ONE = CODE + 2 * BITS
BIG = float(2**20)
BQ = 2 * OWN
BLOCKS = SHARD // BQ
UNIT = 256
MAX_UNITS = 14
STEPS = (7, 6, 5, 4, 3, 2, 1)
CHUNK = 512
PACK_ROWS = 64
SEG_WINDOW = 24
WINDOW = 3 * SHARD
OUT_ROWS = 2 * OWN + OWN // 4
SCALE = math.log2(math.e) / math.sqrt(HD)


def lane_iota(shape, dtype=jnp.int32):
    return lax.broadcasted_iota(dtype, shape, len(shape) - 1)


def turned(x, amount):
    amount %= LANES
    return x if amount == 0 else pltpu.roll(x, amount, 1)


def id_window(seg_ref, ids_ref, sem):
    first_row = jnp.maximum(device_index() * OWN // LANES - SHARD_ROWS, 0)
    base = pl.multiple_of(jnp.minimum(first_row // 8 * 8, SEG_ROWS - SEG_WINDOW), 8)
    return base, pltpu.make_async_copy(seg_ref.at[pl.ds(base, SEG_WINDOW), :], ids_ref, sem)


def device_index():
    return lax.axis_index("seq") * GROUP + lax.axis_index("head")


def row_copies(x_ref, rows_ref, sems):
    count = OWN // PACK_ROWS
    parts = [pl.ds(i * PACK_ROWS, PACK_ROWS) for i in range(count)]
    return [pltpu.make_async_copy(x_ref.at[p, :], rows_ref.at[p, :], sems.at[i]) for i, p in enumerate(parts)]


def swap_matrix():
    source = lax.broadcasted_iota(jnp.int32, (LANES, LANES), 0)
    target = lane_iota((LANES, LANES))
    partner = jnp.where((target % (HD // 2)) < HD // 4, target + HD // 4, target - HD // 4)
    return jnp.where((source == partner) & (target < HD), 1.0, 0.0).astype(jnp.bfloat16)


def row_tools(rows_ref, at, cos, sin, swap):
    lane = lane_iota((PACK_ROWS, LANES))

    def tile(t):
        return rows_ref[at, t * LANES : (t + 1) * LANES]

    def granules(base, count, target):
        t, g = base // LANES, base % LANES
        value = turned(tile(t), target - g)
        if g + 32 * count > LANES:
            cut = target + LANES - g
            value = jnp.where(lane < cut, value, turned(tile(t + 1), target - g))
        return value

    def rope(base):
        x = granules(base, 3, 0)
        other = jnp.dot(x, swap, preferred_element_type=jnp.float32)
        return (x.astype(jnp.float32) * cos + other * sin).astype(jnp.bfloat16)

    return lane, granules, rope


def pack_kernel(
    x_ref, seg_ref, widths_ref, kv_ref, q_ref, cos_ref, sin_ref, code_ref, rows_ref, ids_ref, wide_ref, row_sems, sems
):
    base, ids_copy = id_window(seg_ref, ids_ref, sems.at[0])
    widths_copy = pltpu.make_async_copy(widths_ref, wide_ref, sems.at[1])
    ids_copy.start()
    widths_copy.start()
    copies = row_copies(x_ref, rows_ref, row_sems)
    for copy in copies:
        copy.start()
    first_tok = device_index() * OWN
    rows = lax.broadcasted_iota(jnp.int32, (OWN, 1), 0)
    lanes = lane_iota((1, LANES))
    freq = jnp.zeros((1, LANES), jnp.float32)
    quarter = HD // 4
    for j in range(quarter):
        freq = jnp.where(lanes % quarter == j, float(np.float32(10000.0 ** (-j / quarter))), freq)
    swap = swap_matrix()
    ids_copy.wait()
    widths_copy.wait()
    own = jnp.zeros((OWN, LANES), jnp.float32)
    window = [(ids_ref[r : r + 1, :].astype(jnp.float32), (base + r) * LANES + lanes - first_tok) for r in range(SEG_WINDOW)]
    for ids, place in window:
        own = own + jnp.where(place == rows, ids, 0.0)
    own = jnp.sum(own, axis=1, keepdims=True)
    before = jnp.zeros((OWN, LANES), jnp.float32)
    for ids, place in window:
        before = before + jnp.where((ids == own) & (place < rows), 1.0, 0.0)
    offset = jnp.sum(before, axis=1, keepdims=True)
    samples = lane_iota((1, SAMPLES)).astype(jnp.float32)
    width = jnp.sum(jnp.where(own == samples, wide_ref[...].astype(jnp.float32), 0.0), axis=1, keepdims=True)
    row_pos = jnp.floor((offset + 0.5) / width)
    col_pos = offset - row_pos * width
    angle = jnp.where(lanes < HD // 2, row_pos, col_pos) * freq
    sine = jnp.sin(angle)
    cos_ref[...] = jnp.cos(angle)
    sin_ref[...] = jnp.where((lanes % (HD // 2)) < quarter, -sine, sine)
    ids = own.astype(jnp.int32)
    shift = jnp.clip(jnp.where(lanes < CODE + BITS, lanes - CODE, lanes - CODE - BITS), 0, BITS - 1)
    bit = (ids >> shift) & 1
    code = jnp.where(lanes < CODE + BITS, 1 - bit, bit)
    code = jnp.where(lanes == ONE, 1, jnp.where((lanes >= CODE) & (lanes < ONE), code, 0))
    code_ref[...] = code.astype(jnp.float32).astype(jnp.bfloat16)
    for copy in copies:
        copy.wait()

    def step(i, carry):
        at = pl.ds(pl.multiple_of(i * PACK_ROWS, PACK_ROWS), PACK_ROWS)
        lane, granules, rope = row_tools(rows_ref, at, cos_ref[at, :], sin_ref[at, :], swap)
        for z in range(GROUP):
            q0 = z * 3 * HD
            k0, v0 = D + q0, 2 * D + q0
            for h in range(3):
                kv_ref[z, at, h * LANES : (h + 1) * LANES] = jnp.where(
                    lane < HD, rope(k0 + h * HD), granules(v0 + 32 * h, 1, HD)
                )
            kv_ref[z, at, 3 * LANES : 4 * LANES] = jnp.where(
                lane < HD, granules(v0 + HD, 3, 0), granules(v0 + 2 * HD, 1, HD)
            )
            q2 = rope(q0 + 2 * HD)
            tail = jnp.where(lane < HD, code_ref[at, :], turned(q2, 32))
            kv_ref[z, at, 4 * LANES : 5 * LANES] = jnp.where(lane < CODE, granules(v0 + 2 * HD + 32, 2, 0), tail)
            q_ref[z, at, :LANES] = jnp.where(lane < HD, rope(q0), turned(q2, HD))
            q_ref[z, at, LANES:] = jnp.where(lane < HD, rope(q0 + HD), turned(q2, 64))
        return carry

    lax.fori_loop(0, OWN // PACK_ROWS, step, 0)


def pack(projected, seg_rows, widths_row):
    vmem, hbm = pl.BlockSpec(memory_space=pltpu.VMEM), pl.BlockSpec(memory_space=pltpu.HBM)
    return pl.pallas_call(
        pack_kernel,
        out_shape=[
            jax.ShapeDtypeStruct((GROUP, OWN, KV_LANES), jnp.bfloat16),
            jax.ShapeDtypeStruct((GROUP, OWN, Q_LANES), jnp.bfloat16),
        ],
        in_specs=[hbm] * 3,
        out_specs=[vmem] * 2,
        scratch_shapes=[
            pltpu.VMEM((OWN, LANES), jnp.float32),
            pltpu.VMEM((OWN, LANES), jnp.float32),
            pltpu.VMEM((OWN, LANES), jnp.bfloat16),
            pltpu.VMEM((OWN, 3 * D), jnp.bfloat16),
            pltpu.VMEM((SEG_WINDOW, LANES), jnp.int32),
            pltpu.VMEM((1, SAMPLES), jnp.int32),
            pltpu.SemaphoreType.DMA((OWN // PACK_ROWS,)),
            pltpu.SemaphoreType.DMA((2,)),
        ],
        compiler_params=pltpu.CompilerParams(vmem_limit_bytes=10 * 1024 * 1024),
        name="pack",
    )(projected, seg_rows, widths_row)


def key_ranges(seg_ref, start_ref, count_ref):
    shard = lax.axis_index("seq")

    def ids_of(index):
        return seg_ref[pl.ds(pl.multiple_of(index * SHARD_ROWS, 4), SHARD_ROWS), :].astype(jnp.float32)

    own_ids = ids_of(shard)
    prev_ids = jnp.where(shard > 0, ids_of(jnp.maximum(shard - 1, 0)), -1.0)
    next_ids = jnp.where(shard < SEQ - 1, ids_of(jnp.minimum(shard + 1, SEQ - 1)), -1.0)
    place = lax.broadcasted_iota(jnp.int32, (SHARD_ROWS, LANES), 0) * LANES + lane_iota((SHARD_ROWS, LANES))

    def totals(xs):
        return jnp.sum(jnp.concatenate([jnp.sum(x, axis=0, keepdims=True) for x in xs], axis=0), axis=1, keepdims=True)

    spots = [at for b in range(BLOCKS) for at in (b * BQ, b * BQ + BQ - 1)]
    ids = totals([jnp.where(place == at, own_ids, 0.0) for at in spots])
    ends = []
    for b in range(BLOCKS):
        first, last = ids[2 * b : 2 * b + 1], ids[2 * b + 1 : 2 * b + 2]
        ends.append(jnp.where(own_ids < first, 1.0, 0.0) - jnp.where(prev_ids == first, 1.0, 0.0))
        ends.append(jnp.where(own_ids <= last, 1.0, 0.0) + jnp.where(next_ids == last, 1.0, 0.0))
    ends = totals(ends)
    begin, end = WINDOW, 0
    for b in range(BLOCKS):
        lo = ends[2 * b, 0].astype(jnp.int32) + SHARD
        hi = ends[2 * b + 1, 0].astype(jnp.int32) + SHARD
        start = lo // LANES * LANES
        count = (hi - start + UNIT - 1) // UNIT
        start = jnp.minimum(start, WINDOW - count * UNIT)
        start_ref[b] = start
        count_ref[b] = count
        begin = jnp.minimum(begin, start)
        end = jnp.maximum(end, start + count * UNIT)
    return begin, end


def gather_keys(prev_ref, own_ref, next_ref, seg_ref, kv_ref, v0_ref, start_ref, count_ref):
    begin, end = key_ranges(seg_ref, start_ref, count_ref)
    first_chunk, last_chunk = begin // CHUNK, (end + CHUNK - 1) // CHUNK
    shard_chunks = SHARD // CHUNK

    def copy_from(ref, number):
        low, high = number * shard_chunks, (number + 1) * shard_chunks

        def move(i, carry):
            src = pl.ds(pl.multiple_of((i - low) * CHUNK, CHUNK), CHUNK)
            dst = pl.ds(pl.multiple_of(i * CHUNK, CHUNK), CHUNK)
            lane = lane_iota((CHUNK, LANES))
            parts = []
            for t in range(5):
                value = ref[src, t * LANES : (t + 1) * LANES]
                kv_ref[dst, t * LANES : (t + 1) * LANES] = value
                parts.append(value)
            v0 = jnp.where(lane < 32, turned(parts[0], 32), jnp.where(lane < 64, turned(parts[1], 64), turned(parts[2], 96)))
            v0_ref[dst, :] = jnp.where(lane < HD, v0, jnp.where(lane == HD, 1.0, 0.0).astype(jnp.bfloat16))
            return carry

        lax.fori_loop(jnp.clip(first_chunk, low, high), jnp.clip(last_chunk, low, high), move, 0)

    copy_from(prev_ref, 0)
    copy_from(own_ref, 1)
    copy_from(next_ref, 2)


def attend_kernel(
    prev_ref, own_ref, next_ref, q_ref, seg_ref, out_ref, kv_ref, v0_ref, qa_ref, qc_ref, start_ref, count_ref, *work
):
    gather_keys(prev_ref, own_ref, next_ref, seg_ref, kv_ref, v0_ref, start_ref, count_ref)
    m_refs, o_refs, s_refs = work[:3], work[3:6], work[6:]
    o0_ref, o1_ref, o2_ref = o_refs

    def arrange(b, carry):
        at = pl.ds(pl.multiple_of(b * BQ, BQ), BQ)
        lane = lane_iota((BQ, LANES))
        zero = jnp.zeros((BQ, LANES), jnp.bfloat16)
        t4 = own_ref[at, 4 * LANES :]
        t5 = q_ref[at, :LANES]
        t6 = q_ref[at, LANES:]
        qa_ref[0, at, :] = jnp.where(lane < HD, t5, zero)
        qa_ref[1, at, :] = jnp.where(lane < HD, t6, zero)
        q2 = jnp.where(lane < 32, turned(t5, 32), jnp.where(lane < 64, turned(t6, 64), turned(t4, 96)))
        qa_ref[2, at, :] = jnp.where(lane < HD, q2, zero)
        other = (t4.astype(jnp.float32) - 1.0) * BIG
        qc_ref[at, :] = jnp.where((lane >= CODE) & (lane < ONE), other, 0.0).astype(jnp.bfloat16)
        return carry

    lax.fori_loop(0, BLOCKS, arrange, 0)

    def block(b, carry):
        start, count = start_ref[b], count_ref[b]
        at = pl.ds(pl.multiple_of(b * BQ, BQ), BQ)

        def scores(first_unit, size, j, heads=(0, 1, 2), fresh=False):
            keys = pl.ds(pl.multiple_of(start + first_unit * UNIT + j * size, LANES), size)
            t4 = kv_ref[keys, 4 * LANES :]
            for h in heads:
                k = jnp.concatenate([kv_ref[keys, h * LANES : (h + 1) * LANES], t4], axis=1)
                q = jnp.concatenate([qa_ref[h, at, :], qc_ref[at, :]], axis=1)
                s = lax.dot_general(q, k, (((1,), (1,)), ((), ())), preferred_element_type=jnp.float32)
                for u in range(size // UNIT):
                    s_refs[h][first_unit + j * (size // UNIT) + u] = s[:, u * UNIT : (u + 1) * UNIT]
                top = s[:, :LANES]
                for t in range(1, size // LANES):
                    top = jnp.maximum(top, s[:, t * LANES : (t + 1) * LANES])
                m_refs[h][...] = top if fresh else jnp.maximum(m_refs[h][...], top)

        def blend(first_unit, size, j, heads=(0, 1, 2), fresh=False):
            keys = pl.ds(pl.multiple_of(start + first_unit * UNIT + j * size, LANES), size)
            for h in heads:
                m = jnp.concatenate([m_refs[h][...]] * (UNIT // LANES), axis=1)
                weights = jnp.concatenate(
                    [
                        jnp.exp2(s_refs[h][first_unit + j * (size // UNIT) + u] * SCALE - m).astype(jnp.bfloat16)
                        for u in range(size // UNIT)
                    ],
                    axis=1,
                )
                values = v0_ref[keys, :] if h == 0 else kv_ref[keys, 3 * LANES :]
                blended = jnp.dot(weights, values, preferred_element_type=jnp.float32)
                o_refs[h][...] = blended if fresh else o_refs[h][...] + blended

        def over_keys(what):
            done = 0
            for units in STEPS:
                steps = (count - done) // units
                lax.fori_loop(0, steps, lambda j, c: what(done, units * UNIT, j) or c, 0)
                done = done + steps * units

        def settle(h):
            m_refs[h][...] = jnp.broadcast_to(jnp.max(m_refs[h][...], axis=1, keepdims=True) * SCALE, (BQ, LANES))

        for units in STEPS:

            @pl.when(count == units)
            def _(size=units * UNIT):
                scores(0, size, 0, fresh=True)
                for h in range(3):
                    settle(h)
                blend(0, size, 0, fresh=True)

        @pl.when(count > max(STEPS))
        def _():
            for ref in m_refs:
                ref[...] = jnp.full_like(ref, -3.0e38)
            for ref in o_refs:
                ref[...] = jnp.zeros_like(ref)
            over_keys(scores)
            for h in range(3):
                settle(h)
            over_keys(blend)

        lane = lane_iota((OWN, LANES))
        part = OWN // 4
        part_lane = lane_iota((part, LANES))
        for i in range(BQ // OWN):
            at = slice(i * OWN, (i + 1) * OWN)
            to = b * (BQ // OWN) + i
            o0 = o0_ref[at, :]
            o0 = o0 * (1.0 / o0[:, HD : HD + 1])
            o1 = o1_ref[at, :LANES] * (1.0 / o1_ref[at, LANES:][:, ONE : ONE + 1])
            o2a, o2b = o2_ref[at, :LANES], o2_ref[at, LANES:]
            r2 = 1.0 / o2b[:, ONE : ONE + 1]
            o2a, o2b = o2a * r2, o2b * r2
            out_ref[to, :OWN, :] = jnp.where(lane < HD, o0, o2a).astype(jnp.bfloat16)
            out_ref[to, OWN : 2 * OWN, :] = jnp.where(lane < HD, o1, turned(o2b, 96)).astype(jnp.bfloat16)
            fold = turned(o2b[:part], 96)
            for g in range(1, 4):
                fold = jnp.where(part_lane < 32 * g, fold, turned(o2b[g * part : (g + 1) * part], 32 * g - 32))
            out_ref[to, 2 * OWN :, :] = fold.astype(jnp.bfloat16)
        return carry

    lax.fori_loop(0, BLOCKS, block, 0)


def attend(prev, own, following, queries, seg_rows):
    vmem = pl.BlockSpec(memory_space=pltpu.VMEM)
    return pl.pallas_call(
        attend_kernel,
        out_shape=jax.ShapeDtypeStruct((GROUP, OUT_ROWS, LANES), jnp.bfloat16),
        in_specs=[vmem] * 5,
        out_specs=vmem,
        scratch_shapes=[
            pltpu.VMEM((WINDOW, KV_LANES), jnp.bfloat16),
            pltpu.VMEM((WINDOW, LANES), jnp.bfloat16),
            pltpu.VMEM((3, SHARD, LANES), jnp.bfloat16),
            pltpu.VMEM((SHARD, LANES), jnp.bfloat16),
            pltpu.SMEM((BLOCKS,), jnp.int32),
            pltpu.SMEM((BLOCKS,), jnp.int32),
            *[pltpu.VMEM((BQ, LANES), jnp.float32)] * 4,
            *[pltpu.VMEM((BQ, 2 * LANES), jnp.float32)] * 2,
            *[pltpu.VMEM((MAX_UNITS, BQ, UNIT), jnp.float32)] * 3,
        ],
        compiler_params=pltpu.CompilerParams(vmem_limit_bytes=40 * 1024 * 1024),
        name="attend",
    )(prev, own, following, queries, seg_rows)


def unpack_kernel(in_ref, out_hbm, out_ref, sems):
    group = 3 * LANES
    copies = []
    lane = lane_iota((OWN, LANES))
    part = OWN // 4

    def source(z, i):
        if i < 3:
            return in_ref[z, :OWN, :], i
        if i < 6:
            return in_ref[z, OWN : 2 * OWN, :], i - 3
        return in_ref[z, (i - 6) * OWN : (i - 5) * OWN, :], 3

    for t in range(D // LANES):
        value = None
        for g in range(4):
            z, i = divmod(4 * t + g, 9)
            if i == 8:
                pieces = [turned(in_ref[z, 2 * OWN :, :], 32 * (g - p)) for p in range(4)]
                moved = jnp.concatenate(pieces, axis=0)
            else:
                tile, at = source(z, i)
                moved = turned(tile, 32 * (g - at))
            value = moved if value is None else jnp.where(lane < 32 * g, value, moved)
        out_ref[:, t * LANES : (t + 1) * LANES] = value
        if (t + 1) * LANES % group == 0:
            done = pl.ds((t + 1) * LANES - group, group)
            copies.append(pltpu.make_async_copy(out_ref.at[:, done], out_hbm.at[:, done], sems.at[len(copies)]))
            copies[-1].start()
    for copy in copies:
        copy.wait()


def unpack(returned):
    vmem = pl.BlockSpec(memory_space=pltpu.VMEM)
    return pl.pallas_call(
        unpack_kernel,
        out_shape=jax.ShapeDtypeStruct((OWN, D), jnp.bfloat16),
        in_specs=[vmem],
        out_specs=pl.BlockSpec(memory_space=pltpu.HBM),
        scratch_shapes=[pltpu.VMEM((OWN, D), jnp.bfloat16), pltpu.SemaphoreType.DMA((D // (3 * LANES),))],
        compiler_params=pltpu.CompilerParams(vmem_limit_bytes=8 * 1024 * 1024),
        name="unpack",
    )(returned)


def body(projected, segment_ids, widths):
    seg_rows = segment_ids.reshape(SEG_ROWS, LANES)
    in_hbm = [pltpu.with_memory_space_constraint(a, pltpu.HBM) for a in (projected, seg_rows, widths.reshape(1, SAMPLES))]
    kv, q = pack(*in_hbm)
    kv = lax.all_to_all(kv, "head", 0, 0, tiled=True)
    kv, q = lax.optimization_barrier((kv, q))
    own = kv.reshape(SHARD, KV_LANES)
    up = [(i, (i + 1) % SEQ) for i in range(SEQ)]
    down = [(j, i) for i, j in up]
    prev = lax.ppermute(own, "seq", up)
    following = lax.ppermute(own, "seq", down)
    q = lax.all_to_all(q, "head", 0, 0, tiled=True)
    out = attend(prev, own, following, q.reshape(SHARD, Q_LANES), seg_rows)
    out = lax.all_to_all(out, "head", 0, 0, tiled=True)
    return unpack(out)


def solution(mesh):
    in_specs = (P(("seq", "head"), None), P(), P())
    out_specs = P(("seq", "head"), None)
    return jax.shard_map(body, mesh=mesh, in_specs=in_specs, out_specs=out_specs, check_vma=False)
```
